256 devices in a mesh: node: 16 (over z_hi, y), slab: 16 (over x, z_lo, core).
Axes of the slice: x: 4, y: 4, z: 8 (z_hi: 4, z_lo: 2; z = z_hi * 2 + z_lo), core: 2. Of those that a mesh axis runs over, the one named last changes fastest.
Arguments:
- tensors: float32 [16, 128, 128, 128], P('node', 'slab'), may hold values from -0.375 to 0.375
- ops: float32 [8, 128, 128], replicated, as said below
- assign: int32 [16, 2], replicated, may hold values from 0 to 7
- parent: int32 [16], replicated, may hold values from 0 to 7, as said below
- env: float32 [128, 128], replicated, as said below
Outputs:
- gradient: float32 [16, 128, 128, 128], P('node', None, 'slab')
- energy: float32 [], replicated
The draws below stay inside these ranges and needn't reach their ends.
Inputs may be any that keep to these rules, and one draw needn't show every extreme that they name: parent[0] = 0 and parent[1] = 0; for every level L from 2 to 4, each node of indices 2 ** (L - 1) to 2 ** L - 1 has its parent among indices 2 ** (L - 2) to 2 ** (L - 1) - 1, and each of those is the parent of exactly two of them. Every matrix ops[k] is symmetric. env is symmetric.
All inputs are finite; a program needn't handle non-finite values.
Results may differ from the reference program's by a relative error of at most 0.00012.
Values sent between devices are 32-bit elements; how exact they have to be, the bound alone decides.
A program may use at most 64 MiB of HBM per device.

```python
import jax
import jax.numpy as jnp
from jax import lax

B = 128
LEVELS = 5
OPS = 8
NODES = 16


def symmetric_draw(key, shape):
    base = jax.random.normal(key, shape, jnp.float32)
    sym = (base + jnp.swapaxes(base, -1, -2)) / jnp.sqrt(2.0 * B)
    return sym


def draw_ops(key, part):
    return symmetric_draw(jax.random.fold_in(key, 11), (OPS, B, B))


def draw_env(key, part):
    return symmetric_draw(jax.random.fold_in(key, 23), (B, B))


def draw_parent(key, part):
    pieces = [jnp.zeros((2,), jnp.int32)]
    for level in range(2, LEVELS):
        owners = jnp.repeat(jnp.arange(2 ** (level - 2), 2 ** (level - 1), dtype=jnp.int32), 2)
        pieces.append(jax.random.permutation(jax.random.fold_in(key, 100 + level), owners))
    return jnp.concatenate(pieces).astype(jnp.int32)


def place_ends(result, stream_key, smallest, high):
    longest = result.shape.index(max(result.shape))
    spots = []
    for shift in (0, 1):
        where = [jax.random.randint(jax.random.fold_in(stream_key, axis), (), 0, length) for axis, length in enumerate(result.shape)]
        where[longest] = (where[longest] + shift) % result.shape[longest]
        spots.append(tuple(where))
    return result.at[spots[0]].set(smallest).at[spots[1]].set(high)


def block_levels(stream_key, shape, split, smallest, high):
    def one(dim, shards_of):
        draws = jax.random.uniform(jax.random.fold_in(jax.random.fold_in(stream_key, 6), dim), (shards_of,), jnp.float32, smallest / len(split), high / len(split))
        return jnp.repeat(jnp.exp(draws), shape[dim] // shards_of).reshape((-1,) + (1,) * (len(shape) - dim - 1))

    factor_of = one(*split[0])
    for cut in split[1:]:
        factor_of = factor_of * one(*cut)
    return factor_of


def scatter_about(key, extent, deviation, bound, cuts=(), kind=jnp.bfloat16):
    factor_of = block_levels(key, extent, cuts, -0.22, 0.18) if cuts else 1.0
    entries = jax.random.normal(key, extent, jnp.float32) * deviation * factor_of
    return jnp.minimum(jnp.maximum(entries, -bound), bound).astype(kind)


def setup_inputs(seed: int = 0) -> dict:
    key_of = jax.random.split(jax.random.key(seed), 6)
    return {
        "tensors": scatter_about(key_of[0], (NODES, B, B, B), (B ** -0.75), 0.375, ((0, 16), (1, 16)), jnp.float32),
        "ops": draw_ops(jax.random.fold_in(key_of[5], 71), 0),
        "assign": place_ends(jax.random.randint(key_of[2], (NODES, 2), 0, OPS), jax.random.fold_in(key_of[2], 1), 0, OPS - 1).astype(jnp.int32),
        "parent": draw_parent(jax.random.fold_in(key_of[5], 71), 0),
        "env": draw_env(jax.random.fold_in(key_of[5], 71), 0),
    }


HIGH = lax.Precision.HIGHEST


def tree_links(parent):
    index = jnp.arange(NODES, dtype=jnp.int32)
    linked = (parent[None, :] == index[:, None]) & (index[None, :] >= 1)
    count = jnp.sum(linked.astype(jnp.int32), axis=1)
    left = jnp.min(jnp.where(linked, index[None, :], NODES), axis=1).astype(jnp.int32)
    right = jnp.max(jnp.where(linked, index[None, :], -1), axis=1).astype(jnp.int32)
    return count, left, right


def node_kernel(tensor, left_op, right_op, first, second):
    pair = jnp.einsum('plr,lm->pmr', tensor, first, precision=HIGH)
    pair = jnp.einsum('pmr,rs->pms', pair, second, precision=HIGH)
    along_left = jnp.einsum('plr,lm->pmr', tensor, left_op, precision=HIGH)
    along_right = jnp.einsum('plr,rs->pls', tensor, right_op, precision=HIGH)
    return along_left + along_right + pair


def reference(tensors, ops, assign, parent, env):
    count, left, right = tree_links(parent)
    first_ops = ops[assign[:, 0]]
    second_ops = ops[assign[:, 1]]
    width = tensors.shape[1]
    ups = jnp.zeros((NODES, width, width), jnp.float32)
    left_ops = [None] * NODES
    right_ops = [None] * NODES
    for node in range(NODES - 1, -1, -1):
        left_safe = jnp.minimum(left[node], NODES - 1)
        right_safe = jnp.maximum(right[node], 0)
        left_op = jnp.where(count[node] >= 1, ups[left_safe], first_ops[node])
        right_op = jnp.where(count[node] >= 2, ups[right_safe], second_ops[node])
        left_ops[node] = left_op
        right_ops[node] = right_op
        kern = node_kernel(tensors[node], left_op, right_op, first_ops[node], second_ops[node])
        ups = ups.at[node].set(jnp.einsum('plr,qlr->pq', kern, tensors[node], precision=HIGH))
    energy = jnp.sum(env * ups[0])
    downs = jnp.zeros((NODES, width, width), jnp.float32).at[0].set(env)
    for node in range(NODES // 2):
        tensor = tensors[node]
        moved = jnp.einsum('pq,qlr->plr', downs[node], tensor, precision=HIGH)
        down_left = jnp.einsum('plr,pmr->lm', tensor, moved, precision=HIGH)
        down_right = jnp.einsum('plr,pls->rs', tensor, moved, precision=HIGH)
        left_index = jnp.where(count[node] >= 1, left[node], node).astype(jnp.int32)
        downs = downs.at[left_index].set(jnp.where(count[node] >= 1, down_left, downs[left_index]))
        right_index = jnp.where(count[node] >= 2, right[node], node).astype(jnp.int32)
        downs = downs.at[right_index].set(jnp.where(count[node] >= 2, down_right, downs[right_index]))
    factor = width ** 0.75
    grads = []
    for node in range(NODES):
        kern = node_kernel(tensors[node], left_ops[node], right_ops[node], first_ops[node], second_ops[node])
        grads.append(factor * jnp.einsum('pq,qlr->plr', downs[node], kern, precision=HIGH))
    return jnp.stack(grads), energy
```

```python
import functools

import jax
import jax.numpy as jnp
from jax import lax
from jax.experimental import pallas as pl
from jax.experimental.pallas import tpu as pltpu
from jax.sharding import PartitionSpec as P

NODES = 16
MESH = pl.DeviceIdType.MESH
F32 = jnp.float32
BF16 = jnp.bfloat16

A2A_R, A2A_L, A2A_K, A2A_X, RS_U, RS_D, AG_U, AG_D, SLAB_E, NODE_U, NODE_D, NODE_E = range(12)


def split(x):
    hi = x.astype(BF16)
    return hi, (x - hi.astype(F32)).astype(BF16)


def dot(a, b, nt):
    dims = (((1,), (1 if nt else 0,)), ((), ()))
    return lax.dot_general(a, b, dims, preferred_element_type=F32)


def mm(a, b, nt=False):
    return dot(a[0], b[0], nt) + (dot(a[0], b[1], nt) + dot(a[1], b[0], nt))


def kernel(
    ns, t_ref, ops_ref, env_ref, assign_ref, parent_ref, out_ref, en_ref,
    flat, s_r, s_l, s_k, s_x, t_r, t_l, k_l, x_l,
    th, tl, lh, ll, rh, rl, lth, ltl, rth, rtl,
    up, rs_u, u_row, u_cand, xy_row, xy,
    dp, rs_d, d_row, d_cand, dd_row, dd,
    rs_e, e_row, e_cand, ss, rs,
):
    n = lax.axis_index("node")
    s = lax.axis_index("slab")
    b = env_ref.shape[0]
    w = b // ns
    rows = pl.ds(pl.multiple_of(s * w, w), w)
    leaf = n >= 8

    def block(j):
        return pl.ds(pl.multiple_of(j * w, w), w)

    c0 = jnp.where(n >= 4, 8, jnp.where(n >= 2, 4, jnp.where(n >= 1, 2, 1)))
    c1 = jnp.where(n >= 1, 2 * c0, 2)
    p0 = jnp.where(n >= 8, 4, jnp.where(n >= 4, 2, jnp.where(n >= 2, 1, 0)))
    p1 = jnp.where(n >= 2, 2 * p0, 1)

    barrier = pltpu.get_barrier_semaphore()

    def greet_slab(k, c):
        pl.semaphore_signal(barrier, inc=1, device_id=(n, lax.rem(s + k, ns)), device_id_type=MESH)
        return c

    def greet_node(k, c):
        pl.semaphore_signal(barrier, inc=1, device_id=(lax.rem(n + k, NODES), s), device_id_type=MESH)
        return c

    lax.fori_loop(1, ns, greet_slab, 0)
    lax.fori_loop(1, NODES, greet_node, 0)

    def slab_copy(q, src, dst, to, frm):
        return pltpu.make_async_remote_copy(
            src_ref=src, dst_ref=dst, send_sem=ss.at[q, to], recv_sem=rs.at[q, frm],
            device_id=(n, to), device_id_type=MESH,
        )

    def slab_start(q, src_of, dst):
        def go(k, c):
            j = lax.rem(s + k, ns)
            slab_copy(q, src_of(j), dst, j, s).start()
            return c

        lax.fori_loop(1, ns, go, 0)

    def slab_wait(q, dst_of):
        def go(k, c):
            i = lax.rem(s + k, ns)
            slab_copy(q, dst_of(i), dst_of(i), i, i).wait_recv()
            return c

        lax.fori_loop(1, ns, go, 0)

    def slab_drain(q, src_of):
        def go(k, c):
            j = lax.rem(s + k, ns)
            slab_copy(q, src_of(j), src_of(j), j, s).wait_send()
            return c

        lax.fori_loop(1, ns, go, 0)

    def node_copy(q, src, dst, to, frm):
        return pltpu.make_async_remote_copy(
            src_ref=src, dst_ref=dst, send_sem=ss.at[q, to], recv_sem=rs.at[q, frm],
            device_id=(to, s), device_id_type=MESH,
        )

    def node_start(q, src, dst, lo, hi):
        def go(m, c):
            node_copy(q, src, dst, m, n).start()
            return c

        lax.fori_loop(lo, hi, go, 0)

    def node_wait(q, dst_of, lo, hi):
        def go(m, c):
            node_copy(q, dst_of(m), dst_of(m), m, m).wait_recv()
            return c

        lax.fori_loop(lo, hi, go, 0)

    def node_drain(q, src, lo, hi):
        def go(m, c):
            node_copy(q, src, src, m, n).wait_send()
            return c

        lax.fori_loop(lo, hi, go, 0)

    def relayout(src, dst):
        for i in range(b):
            dst[i] = src[pl.ds(i, w, stride=b), :]

    def a2a_start(q, src, dst):
        slab_start(q, lambda j: src.at[block(j)], dst.at[:, rows, :])
        dst[:, rows, :] = src[rows]

    def a2a_wait(q, dst):
        slab_wait(q, lambda i: dst.at[:, block(i), :])

    def a2a_drain(q, src):
        slab_drain(q, lambda j: src.at[block(j)])

    def both(h, l, i):
        return h[i * b : (i + 1) * b, :], l[i * b : (i + 1) * b, :]

    def sandwich(h, l, x, add=None):
        total = jnp.zeros((b, b), F32)
        for i in range(w):
            m = both(h, l, i)
            moved = mm(m, x)
            if add is not None:
                add[i] = add[i] + moved
            total = total + mm(split(moved), m, nt=True)
        return total

    def store_split(h, l, i, x):
        h[i * b : (i + 1) * b, :], l[i * b : (i + 1) * b, :] = split(x)

    op_p = split(ops_ref[assign_ref[n, 0]])
    op_q = split(ops_ref[assign_ref[n, 1]])

    @pl.when(n < 8)
    def _():
        for i in range(w):
            flat[i * b : (i + 1) * b, :] = t_ref[i * b : (i + 1) * b, :].T
        relayout(flat, s_r)

    relayout(t_ref, s_l)
    pl.semaphore_wait(barrier, ns - 1 + NODES - 1)

    @pl.when(n < 8)
    def _():
        a2a_start(A2A_R, s_r, t_r)

    a2a_start(A2A_L, s_l, t_l)
    for i in range(w):
        store_split(th, tl, i, t_ref[i * b : (i + 1) * b, :])
    for i in range(w):
        t = t_ref[i * b : (i + 1) * b, :]
        tq = mm(both(th, tl, i), op_q)
        v = jnp.where(leaf, t + tq, tq)
        flat[i * b : (i + 1) * b, :] = mm(op_p, split(v)) + jnp.where(leaf, tq, 0.0)
    relayout(flat, s_k)
    a2a_start(A2A_K, s_k, k_l)

    @pl.when(n < 8)
    def _():
        a2a_wait(A2A_R, t_r)
        for i in range(w):
            store_split(rth, rtl, i, t_r[i].T)
            store_split(rh, rl, i, t_r[i])

    a2a_wait(A2A_L, t_l)
    for i in range(w):
        store_split(lh, ll, i, t_l[i])

    @pl.when(n < 8)
    def _():
        for i in range(w):
            store_split(lth, ltl, i, t_l[i].T)

    def pair_square():
        a2a_wait(A2A_K, k_l)
        total = jnp.zeros((b, b), F32)
        for i in range(w):
            total = total + mm(split(k_l[i]), both(lh, ll, i), nt=True)
        up[...] = total

    def family(m):
        first = jnp.int32(NODES)
        last = jnp.int32(0)
        for k in range(NODES - 1, 0, -1):
            hit = parent_ref[k] == m
            first = jnp.where(hit, k, first)
        for k in range(1, NODES):
            last = jnp.where(parent_ref[k] == m, k, last)
        return jnp.minimum(first, NODES - 1), last

    def receive_d():
        node_wait(NODE_D, lambda m: d_cand.at[m], p0, p1)
        mine = parent_ref[n]
        first, _ = family(mine)
        side = jnp.where(first == n, 0, 1)
        dd_row[...] = d_cand[mine, side]
        slab_start(AG_D, lambda j: dd_row, dd.at[rows, :])
        dd[rows, :] = dd_row[...]
        slab_wait(AG_D, lambda i: dd.at[block(i), :])

    def send_d():
        d = split(dd[...])
        dp[0] = sandwich(rth, rtl, d)
        dp[1] = sandwich(lth, ltl, d)
        slab_start(RS_D, lambda j: dp.at[:, block(j), :], rs_d.at[s])
        rs_d[s] = dp[:, rows, :]
        slab_wait(RS_D, lambda i: rs_d.at[i])
        total = rs_d[0]
        for k in range(1, ns):
            total = total + rs_d[k]
        d_row[...] = total
        node_start(NODE_D, d_row, d_cand.at[n], c0, c1)

    def send_u():
        slab_start(RS_U, lambda j: up.at[block(j), :], rs_u.at[s])
        rs_u[s] = up[rows, :]
        slab_wait(RS_U, lambda i: rs_u.at[i])
        total = rs_u[0]
        for k in range(1, ns):
            total = total + rs_u[k]
        u_row[...] = total
        node_start(NODE_U, u_row, u_cand.at[n], p0, p1)

    def receive_u():
        first, last = family(n)
        node_wait(NODE_U, lambda m: u_cand.at[m], c0, c1)
        xy_row[0] = u_cand[first]
        second = u_cand[last]
        xy_row[1] = jnp.where(n == 0, ops_ref[assign_ref[n, 1], rows, :], second)
        slab_start(AG_U, lambda j: xy_row, xy.at[:, rows, :])
        xy[:, rows, :] = xy_row[...]
        slab_wait(AG_U, lambda i: xy.at[:, block(i), :])

    def move_left(x):
        for i in range(w):
            flat[i * b : (i + 1) * b, :] = mm(x, both(th, tl, i))
        relayout(flat, s_x)
        a2a_start(A2A_X, s_x, x_l)

    def send_energy(square):
        terms = dd[...] * square
        total = terms[0:w, :]
        for k in range(1, ns):
            total = total + terms[k * w : (k + 1) * w, :]
        rs_e[s] = total
        slab_start(SLAB_E, lambda j: rs_e.at[s], rs_e.at[s])

    def share_energy():
        slab_wait(SLAB_E, lambda i: rs_e.at[i])
        total = rs_e[0]
        for k in range(1, ns):
            total = total + rs_e[k]
        e_cand[n] = total

        def go(k, c):
            m = lax.rem(n + k, NODES)
            node_copy(NODE_E, e_cand.at[n], e_cand.at[n], m, n).start()
            return c

        lax.fori_loop(1, NODES, go, 0)

    def climb():
        receive_u()
        x = split(xy[0])
        y = split(xy[1])
        up[...] = up[...] + sandwich(rh, rl, x) + sandwich(lh, ll, y, add=k_l)
        send_u()
        move_left(x)

    @pl.when(leaf)
    def _():
        pair_square()
        send_u()
        receive_d()

    @pl.when((n >= 4) & (n < 8))
    def _():
        pair_square()
        climb()
        receive_d()
        send_d()

    @pl.when((n >= 1) & (n < 4))
    def _():
        receive_d()
        send_d()
        pair_square()

        @pl.when(n == 1)
        def _():
            send_energy(up[...])
            share_energy()

        climb()

        @pl.when(n > 1)
        def _():
            send_energy(up[...])
            share_energy()

    @pl.when(n == 0)
    def _():
        dd[...] = env_ref[...]
        send_d()
        pair_square()
        send_energy(up[...] + sandwich(lh, ll, op_q, add=k_l))
        share_energy()
        receive_u()
        move_left(split(xy[0]))

    factor = b**0.75
    d = split(dd[...])

    @pl.when(n < 8)
    def _():
        a2a_wait(A2A_X, x_l)

    for i in range(w):
        part = k_l[i] + jnp.where(n < 8, x_l[i], 0.0)
        out_ref[i] = factor * mm(d, split(part))

    def energy_wait(m, c):
        @pl.when(m != n)
        def _():
            node_copy(NODE_E, e_cand.at[m], e_cand.at[m], m, m).wait_recv()

        return c

    lax.fori_loop(0, 4, energy_wait, 0)
    total = (e_cand[0] + e_cand[1]) + (e_cand[2] + e_cand[3])
    en_ref[...] = jnp.sum(total, axis=(0, 1), keepdims=True)

    a2a_drain(A2A_L, s_l)
    a2a_drain(A2A_K, s_k)

    @pl.when(n < 8)
    def _():
        a2a_drain(A2A_R, s_r)
        a2a_drain(A2A_X, s_x)
        slab_drain(RS_D, lambda j: dp.at[:, block(j), :])
        node_drain(NODE_D, d_row, c0, c1)
        slab_drain(AG_U, lambda j: xy_row)

    @pl.when(n >= 1)
    def _():
        slab_drain(RS_U, lambda j: up.at[block(j), :])
        node_drain(NODE_U, u_row, p0, p1)
        slab_drain(AG_D, lambda j: dd_row)

    @pl.when(n < 4)
    def _():
        slab_drain(SLAB_E, lambda j: rs_e.at[s])

        def go(k, c):
            m = lax.rem(n + k, NODES)
            node_copy(NODE_E, e_cand.at[n], e_cand.at[n], m, n).wait_send()
            return c

        lax.fori_loop(1, NODES, go, 0)


def per_device(ns, tensors, ops, assign, parent, env):
    b = env.shape[0]
    w = b // ns
    full = pltpu.VMEM((b, w, b), F32)
    form = pltpu.VMEM((w, b, b), F32)
    half = pltpu.VMEM((w * b, b), BF16)
    square = pltpu.VMEM((b, b), F32)
    slots = max(ns, NODES)
    vmem = pl.BlockSpec(memory_space=pltpu.VMEM)
    smem = pl.BlockSpec(memory_space=pltpu.SMEM)
    grad, energy = pl.pallas_call(
        functools.partial(kernel, ns),
        out_shape=(jax.ShapeDtypeStruct((w, b, b), F32), jax.ShapeDtypeStruct((1, 1), F32)),
        in_specs=[vmem, vmem, vmem, smem, smem],
        out_specs=(vmem, vmem),
        scratch_shapes=[
            pltpu.VMEM((w * b, b), F32), full, full, full, full, form, form, form, form,
            half, half, half, half, half, half, half, half, half, half,
            square, pltpu.VMEM((ns, w, b), F32), pltpu.VMEM((w, b), F32),
            pltpu.VMEM((NODES, w, b), F32), pltpu.VMEM((2, w, b), F32), pltpu.VMEM((2, b, b), F32),
            pltpu.VMEM((2, b, b), F32), pltpu.VMEM((ns, 2, w, b), F32), pltpu.VMEM((2, w, b), F32),
            pltpu.VMEM((NODES, 2, w, b), F32), pltpu.VMEM((w, b), F32), square,
            pltpu.VMEM((ns, w, b), F32), pltpu.VMEM((w, b), F32), pltpu.VMEM((NODES, w, b), F32),
            pltpu.SemaphoreType.DMA((12, slots)), pltpu.SemaphoreType.DMA((12, slots)),
        ],
        compiler_params=pltpu.CompilerParams(collective_id=0, has_side_effects=True),
    )(tensors.reshape(w * b, b), ops, env, assign, parent)
    return grad.transpose(1, 0, 2)[None], energy[0, 0]


def solution(mesh):
    return jax.shard_map(
        functools.partial(per_device, mesh.shape["slab"]),
        mesh=mesh,
        in_specs=(P("node", "slab", None, None), P(), P(), P(), P()),
        out_specs=(P("node", None, "slab", None), P()),
        check_vma=False,
    )
```

```python
import functools

import jax
import jax.numpy as jnp
from jax import lax
from jax.experimental import pallas as pl
from jax.experimental.pallas import tpu as pltpu
from jax.sharding import PartitionSpec as P

NODES = 16
MESH = pl.DeviceIdType.MESH
F32 = jnp.float32
BF16 = jnp.bfloat16

A2A_R, A2A_L, A2A_K, A2A_X, RS_U, RS_D, AG_U, AG_D, SLAB_E, NODE_U, NODE_D, NODE_E, NODE_F = range(13)


def split(x):
    hi = x.astype(BF16)
    return hi, (x - hi.astype(F32)).astype(BF16)


def beside(x):
    return jnp.concatenate(split(x), axis=1)


def above(x):
    return jnp.concatenate(split(x), axis=0)


def dot(a, b, nt=False, precision=None):
    dims = (((1,), (1 if nt else 0,)), ((), ()))
    return lax.dot_general(a, b, dims, preferred_element_type=F32, precision=precision)


def exact(a, b, nt=False):
    return dot(a, b, nt, lax.Precision.HIGHEST)


def quarters(x):
    h, w = x.shape[0] // 2, x.shape[1] // 2
    return (x[:h, :w] + x[:h, w:]) + (x[h:, :w] + x[h:, w:])


def product(x, y):
    return quarters(dot(x, y))


def kernel(
    ns, t_hbm, ops_hbm, env_hbm, assign_ref, parent_ref, out_hbm, en_ref,
    t_ref, ops_ref, env_ref, out_ref, in_sem, out_sem,
    flat, s_r, s_l, s_k, s_x, t_r, t_l, k_l, x_l, rt, lt,
    tc, lc, rc, ltc, rtc, lp, rp, ltp, rtp, kc,
    up, rs_u, u_row, u_cand, xy_row, xy,
    dp, rs_d, d_row, d_cand, dd_row, dd,
    rs_e, e_row, e_cand, e_all, ss, rs,
):
    n = lax.axis_index("node")
    s = lax.axis_index("slab")
    b = env_ref.shape[0]
    w = b // ns
    rows = pl.ds(pl.multiple_of(s * w, w), w)
    leaf = n >= 8

    loads = [
        pltpu.make_async_copy(t_hbm, t_ref, in_sem.at[0]),
        pltpu.make_async_copy(ops_hbm, ops_ref, in_sem.at[1]),
        pltpu.make_async_copy(env_hbm, env_ref, in_sem.at[2]),
    ]
    for load in loads:
        load.start()

    def block(j):
        return pl.ds(pl.multiple_of(j * w, w), w)

    c0 = jnp.where(n >= 4, 8, jnp.where(n >= 2, 4, jnp.where(n >= 1, 2, 1)))
    c1 = jnp.where(n >= 8, 8, jnp.where(n >= 1, 2 * c0, 2))
    p0 = jnp.where(n >= 8, 4, jnp.where(n >= 4, 2, jnp.where(n >= 2, 1, 0)))
    p1 = jnp.where(n >= 2, 2 * p0, jnp.where(n >= 1, 1, 0))

    barrier = pltpu.get_barrier_semaphore()

    def greet_slab(k, c):
        pl.semaphore_signal(barrier, inc=1, device_id=(n, lax.rem(s + k, ns)), device_id_type=MESH)
        return c

    def greet_node(m, c):
        pl.semaphore_signal(barrier, inc=1, device_id=(m, s), device_id_type=MESH)
        return c

    lax.fori_loop(1, ns, greet_slab, 0)
    lax.fori_loop(p0, p1, greet_node, 0)
    lax.fori_loop(c0, c1, greet_node, 0)

    @pl.when((n == 2) | (n == 3))
    def _():
        greet_node(5 - n, 0)

    pair_of_two = jnp.where((n == 2) | (n == 3), 1, 0)
    greetings = (ns - 1) + (p1 - p0) + (c1 - c0) + pair_of_two

    def peer(k):
        return lax.rem(s + 1 + lax.rem(k + ns // 2 - 2, ns - 1), ns)

    def slab_copy(q, src, dst, to, frm):
        return pltpu.make_async_remote_copy(
            src_ref=src, dst_ref=dst, send_sem=ss.at[q, to], recv_sem=rs.at[q, frm],
            device_id=(n, to), device_id_type=MESH,
        )

    def slab_start(q, src_of, dst):
        def go(k, c):
            j = peer(k)
            slab_copy(q, src_of(j), dst, j, s).start()
            return c

        lax.fori_loop(1, ns, go, 0)

    def slab_wait(q, dst_of):
        def go(k, c):
            i = lax.rem(s + k, ns)
            slab_copy(q, dst_of(i), dst_of(i), i, i).wait_recv()
            return c

        lax.fori_loop(1, ns, go, 0)

    def slab_drain(q, src_of):
        def go(k, c):
            j = lax.rem(s + k, ns)
            slab_copy(q, src_of(j), src_of(j), j, s).wait_send()
            return c

        lax.fori_loop(1, ns, go, 0)

    def node_copy(q, src, dst, to, frm):
        return pltpu.make_async_remote_copy(
            src_ref=src, dst_ref=dst, send_sem=ss.at[q, to], recv_sem=rs.at[q, frm],
            device_id=(to, s), device_id_type=MESH,
        )

    def node_start(q, src, dst, lo, hi):
        def go(m, c):
            node_copy(q, src, dst, m, n).start()
            return c

        lax.fori_loop(lo, hi, go, 0)

    def node_wait(q, dst_of, lo, hi):
        def go(m, c):
            node_copy(q, dst_of(m), dst_of(m), m, m).wait_recv()
            return c

        lax.fori_loop(lo, hi, go, 0)

    def node_drain(q, src, lo, hi):
        def go(m, c):
            node_copy(q, src, src, m, n).wait_send()
            return c

        lax.fori_loop(lo, hi, go, 0)

    def relayout(src, dst):
        for i in range(b):
            dst[i] = src[pl.ds(i, w, stride=b), :]

    def a2a_start(q, src, dst):
        slab_start(q, lambda j: src.at[block(j)], dst.at[:, rows, :])
        dst[:, rows, :] = src[rows]

    def a2a_wait(q, dst):
        slab_wait(q, lambda i: dst.at[:, block(i), :])

    def a2a_drain(q, src):
        slab_drain(q, lambda j: src.at[block(j)])

    def part(i):
        return slice(i * b, (i + 1) * b)

    def store_forms(cat, pair, i, x):
        h, l = split(x)
        cat[part(i), :] = jnp.concatenate([h, l], axis=1)
        lanes = part(i % 2)
        pair[i // 2, 0:b, lanes] = h
        pair[i // 2, b : 2 * b, lanes] = l

    def sandwich(cat, pair, x, add=None):
        side = beside(x)
        weights = jnp.concatenate([side, side], axis=0)
        total = jnp.zeros((2 * b, 2 * b), F32)
        for i in range(0, w, 2):
            moved = []
            for k in (i, i + 1):
                both = dot(cat[part(k), :], weights)
                both = both[:, :b] + both[:, b:]
                if add is not None:
                    add[k] = add[k] + both
                moved.append(above(both))
            total = total + dot(jnp.concatenate(moved, axis=1), pair[i // 2], nt=True)
        return quarters(total)

    def exact_sandwich(m, x):
        total = jnp.zeros((b, b), F32)
        for i in range(w):
            total = total + exact(exact(m[i], x), m[i], nt=True)
        return total

    def family(m):
        first = jnp.int32(NODES - 1)
        last = jnp.int32(0)
        for k in range(NODES - 1, 0, -1):
            first = jnp.where(parent_ref[k] == m, k, first)
        for k in range(1, NODES):
            last = jnp.where(parent_ref[k] == m, k, last)
        return first, last

    left_child, right_child = family(n)
    mine = parent_ref[n]
    eldest, _ = family(mine)
    side_of = jnp.where(eldest == n, 0, 1)
    first_id = assign_ref[0, n]
    second_id = assign_ref[1, n]

    loads[0].wait()

    @pl.when(n < 8)
    def _():
        for i in range(w):
            flat[part(i), :] = t_ref[part(i), :].T
        relayout(flat, s_r)

    relayout(t_ref, s_l)
    pl.semaphore_wait(barrier, greetings)

    @pl.when(n < 8)
    def _():
        a2a_start(A2A_R, s_r, t_r)

    a2a_start(A2A_L, s_l, t_l)
    loads[1].wait()
    loads[2].wait()
    op_p = ops_ref[first_id]
    op_q = ops_ref[second_id]
    for i in range(w):
        t = t_ref[part(i), :]
        tq = exact(t, op_q)
        v = jnp.where(leaf, t + tq, tq)
        flat[part(i), :] = exact(op_p, v) + jnp.where(leaf, tq, 0.0)
    relayout(flat, s_k)
    a2a_start(A2A_K, s_k, k_l)

    def right_forms():
        a2a_wait(A2A_R, t_r)
        for i in range(w):
            x = t_r[i].T
            rt[i] = x
            store_forms(rtc, rtp, i, x)
        for i in range(w):
            store_forms(rc, rp, i, t_r[i])

    def left_forms():
        a2a_wait(A2A_L, t_l)
        for i in range(w):
            x = t_l[i].T
            lt[i] = x
            store_forms(ltc, ltp, i, x)
        for i in range(w):
            store_forms(lc, lp, i, t_l[i])

    def own_forms():
        for i in range(w):
            tc[part(i), :] = beside(t_ref[part(i), :])

    def pair_square():
        a2a_wait(A2A_K, k_l)
        total = jnp.zeros((b, b), F32)
        for i in range(w):
            total = total + exact(k_l[i], t_l[i], nt=True)
        up[...] = total

    def pick_d():
        node_wait(NODE_D, lambda m: d_cand.at[m], p0, p1)
        dd_row[...] = d_cand[mine, side_of]
        slab_start(AG_D, lambda j: dd_row, dd.at[rows, :])
        dd[rows, :] = dd_row[...]

    def gather_d():
        slab_wait(AG_D, lambda i: dd.at[block(i), :])

    def push_d():
        slab_start(RS_D, lambda j: dp.at[:, block(j), :], rs_d.at[s])
        rs_d[s] = dp[:, rows, :]

    def square_d():
        d = dd[...]
        dp[0] = sandwich(rtc, rtp, d)
        dp[1] = sandwich(ltc, ltp, d)
        push_d()

    def send_d():
        slab_wait(RS_D, lambda i: rs_d.at[i])
        total = rs_d[0]
        for k in range(1, ns):
            total = total + rs_d[k]
        d_row[...] = total
        node_start(NODE_D, d_row, d_cand.at[n], c0, c1)

    def push_u():
        slab_start(RS_U, lambda j: up.at[block(j), :], rs_u.at[s])
        rs_u[s] = up[rows, :]

    def send_u():
        slab_wait(RS_U, lambda i: rs_u.at[i])
        total = rs_u[0]
        for k in range(1, ns):
            total = total + rs_u[k]
        u_row[...] = total
        node_start(NODE_U, u_row, u_cand.at[n], p0, p1)

    def pick_u():
        node_wait(NODE_U, lambda m: u_cand.at[m], c0, c1)
        xy_row[0] = u_cand[left_child]
        second = u_cand[right_child]
        xy_row[1] = jnp.where(n == 0, ops_ref[second_id, rows, :], second)
        slab_start(AG_U, lambda j: xy_row, xy.at[:, rows, :])
        xy[:, rows, :] = xy_row[...]

    def gather_u():
        slab_wait(AG_U, lambda i: xy.at[:, block(i), :])

    def square_u():
        up[...] = up[...] + (sandwich(rc, rp, xy[0]) + sandwich(lc, lp, xy[1], add=k_l))
        push_u()

    def move_left():
        x = above(xy[0])
        for i in range(w):
            flat[part(i), :] = product(x, tc[part(i), :])
        relayout(flat, s_x)
        a2a_start(A2A_X, s_x, x_l)

    def push_energy(square):
        terms = dd[...] * square
        total = terms[0:w, :]
        for k in range(1, ns):
            total = total + terms[k * w : (k + 1) * w, :]
        rs_e[s] = total
        slab_start(SLAB_E, lambda j: rs_e.at[s], rs_e.at[s])

    def own_energy():
        slab_wait(SLAB_E, lambda i: rs_e.at[i])
        total = rs_e[0]
        for k in range(1, ns):
            total = total + rs_e[k]
        return total

    def wait_total(frm):
        node_wait(NODE_F, lambda m: e_all, frm, frm + 1)

    @pl.when(leaf)
    def _():
        a2a_wait(A2A_L, t_l)
        pair_square()
        push_u()
        send_u()
        pick_d()
        gather_d()

    @pl.when((n >= 4) & (n < 8))
    def _():
        right_forms()
        left_forms()
        pair_square()
        own_forms()
        pick_u()
        gather_u()
        square_u()
        send_u()
        move_left()
        pick_d()
        gather_d()
        square_d()
        send_d()
        wait_total(2)
        node_start(NODE_F, e_all, e_all, 2 * n, 2 * n + 2)

    @pl.when((n == 2) | (n == 3))
    def _():
        right_forms()
        left_forms()
        pair_square()
        own_forms()
        pick_d()
        gather_d()
        square_d()
        pick_u()
        send_d()
        gather_u()
        square_u()
        send_u()
        push_energy(up[...])
        move_left()
        e_row[...] = own_energy()
        e_cand[n] = e_row[...]
        node_start(NODE_E, e_row, e_cand.at[n], 5 - n, 6 - n)
        node_wait(NODE_E, lambda m: e_cand.at[m], 1, 2)
        node_wait(NODE_E, lambda m: e_cand.at[m], 5 - n, 6 - n)
        e_all[...] = e_cand[1] + (e_cand[2] + e_cand[3])

        @pl.when(n == 2)
        def _():
            node_start(NODE_F, e_all, e_all, 4, 8)
            node_start(NODE_F, e_all, e_all, 1, 2)

    @pl.when(n == 1)
    def _():
        right_forms()
        left_forms()
        pick_d()
        gather_d()
        d = dd[...]
        dp[0] = exact_sandwich(rt, d)
        dp[1] = exact_sandwich(lt, d)
        push_d()
        send_d()
        pair_square()
        push_energy(up[...])
        own_forms()
        own = own_energy()
        node_wait(NODE_E, lambda m: e_cand.at[m], 0, 1)
        e_row[...] = own + e_cand[0]
        node_start(NODE_E, e_row, e_cand.at[n], 2, 4)
        pick_u()
        gather_u()
        square_u()
        send_u()
        move_left()
        wait_total(2)
        node_start(NODE_F, e_all, e_all, 0, 1)

    @pl.when(n == 0)
    def _():
        dd[...] = env_ref[...]
        right_forms()
        dp[0] = exact_sandwich(rt, env_ref[...])
        dp[1] = jnp.zeros((b, b), F32)
        push_d()
        send_d()
        left_forms()
        pair_square()
        push_energy(up[...] + sandwich(lc, lp, op_q, add=k_l))
        e_row[...] = own_energy()
        node_start(NODE_E, e_row, e_cand.at[n], 1, 2)
        own_forms()
        pick_u()
        gather_u()
        move_left()
        wait_total(1)

    factor = b**0.75

    @pl.when(n < 8)
    def _():
        a2a_wait(A2A_X, x_l)

    for i in range(w):
        kc[part(i), :] = beside(k_l[i] + jnp.where(n < 8, x_l[i], 0.0))
    chunk = b // 2
    puts = []
    for h in range(2):
        d = above(dd[h * chunk : (h + 1) * chunk, :] * factor)
        for i in range(w):
            out_ref[pl.ds(h * chunk * w + i, chunk, stride=w), :] = product(d, kc[part(i), :])
        span = pl.ds(h * chunk * w, chunk * w)
        puts.append(pltpu.make_async_copy(out_ref.at[span, :], out_hbm.at[span, :], out_sem.at[h]))
        puts[h].start()

    @pl.when(leaf)
    def _():
        wait_total(n // 2)

    en_ref[...] = jnp.sum(e_all[...], axis=(0, 1), keepdims=True)

    a2a_drain(A2A_L, s_l)
    a2a_drain(A2A_K, s_k)

    @pl.when(n < 8)
    def _():
        a2a_drain(A2A_R, s_r)
        a2a_drain(A2A_X, s_x)
        slab_drain(RS_D, lambda j: dp.at[:, block(j), :])
        node_drain(NODE_D, d_row, c0, c1)
        slab_drain(AG_U, lambda j: xy_row)

    @pl.when(n >= 1)
    def _():
        slab_drain(RS_U, lambda j: up.at[block(j), :])
        node_drain(NODE_U, u_row, p0, p1)
        slab_drain(AG_D, lambda j: dd_row)

    @pl.when(n < 4)
    def _():
        slab_drain(SLAB_E, lambda j: rs_e.at[s])
        node_drain(NODE_E, e_row, jnp.where(n >= 2, 5 - n, n + 1), jnp.where(n >= 2, 6 - n, 2 * n + 2))

    @pl.when(n == 1)
    def _():
        node_drain(NODE_F, e_all, 0, 1)

    @pl.when(n == 2)
    def _():
        node_drain(NODE_F, e_all, 4, 8)
        node_drain(NODE_F, e_all, 1, 2)

    @pl.when((n >= 4) & (n < 8))
    def _():
        node_drain(NODE_F, e_all, 2 * n, 2 * n + 2)

    for put in puts:
        put.wait()


def per_device(ns, tensors, ops, assign, parent, env):
    b = env.shape[0]
    w = b // ns
    stack = pltpu.VMEM((w * b, b), F32)
    full = pltpu.VMEM((b, w, b), F32)
    form = pltpu.VMEM((w, b, b), F32)
    cat = pltpu.VMEM((w * b, 2 * b), BF16)
    pair = pltpu.VMEM((w // 2, 2 * b, 2 * b), BF16)
    square = pltpu.VMEM((b, b), F32)
    slab = pltpu.VMEM((w, b), F32)
    two = pltpu.VMEM((2, w, b), F32)
    slots = max(ns, NODES)
    smem = pl.BlockSpec(memory_space=pltpu.SMEM)
    hbm = pl.BlockSpec(memory_space=pl.ANY)
    grad, energy = pl.pallas_call(
        functools.partial(kernel, ns),
        out_shape=(jax.ShapeDtypeStruct((b * w, b), F32), jax.ShapeDtypeStruct((1, 1), F32)),
        in_specs=[hbm, hbm, hbm, smem, smem],
        out_specs=(hbm, pl.BlockSpec(memory_space=pltpu.VMEM)),
        scratch_shapes=[
            stack, pltpu.VMEM(ops.shape, F32), square, stack,
            pltpu.SemaphoreType.DMA((3,)), pltpu.SemaphoreType.DMA((2,)),
            stack, full, full, full, full, form, form, form, form, form, form,
            cat, cat, cat, cat, cat, pair, pair, pair, pair, cat,
            square, pltpu.VMEM((ns, w, b), F32), slab, pltpu.VMEM((NODES, w, b), F32), two, pltpu.VMEM((2, b, b), F32),
            pltpu.VMEM((2, b, b), F32), pltpu.VMEM((ns, 2, w, b), F32), two,
            pltpu.VMEM((NODES, 2, w, b), F32), slab, square,
            pltpu.VMEM((ns, w, b), F32), slab, pltpu.VMEM((NODES, w, b), F32), slab,
            pltpu.SemaphoreType.DMA((13, slots)), pltpu.SemaphoreType.DMA((13, slots)),
        ],
        compiler_params=pltpu.CompilerParams(collective_id=0, has_side_effects=True),
    )(tensors.reshape(w * b, b), ops, env, assign.T, parent)
    return grad.reshape(1, b, w, b), energy[0, 0]


def solution(mesh):
    return jax.shard_map(
        functools.partial(per_device, mesh.shape["slab"]),
        mesh=mesh,
        in_specs=(P("node", "slab", None, None), P(), P(), P(), P()),
        out_specs=(P("node", None, "slab", None), P()),
        check_vma=False,
    )
```

```python
import functools

import jax
import jax.numpy as jnp
from jax import lax
from jax.experimental import pallas as pl
from jax.experimental.pallas import tpu as pltpu
from jax.sharding import PartitionSpec as P

NODES = 16
MESH = pl.DeviceIdType.MESH
F32 = jnp.float32
BF16 = jnp.bfloat16

A2A_R, A2A_L, A2A_K, A2A_X, RS_U, RS_D, AG_U, AG_D, SLAB_E, NODE_U, NODE_D, NODE_E, NODE_F, A2A_Z, MERGE, MERGE2 = range(16)


def split(x):
    hi = x.astype(BF16)
    return hi, (x - hi.astype(F32)).astype(BF16)


def beside(x):
    return jnp.concatenate(split(x), axis=1)


def above(x):
    return jnp.concatenate(split(x), axis=0)


def dot(a, b, nt=False, precision=None):
    dims = (((1,), (1 if nt else 0,)), ((), ()))
    return lax.dot_general(a, b, dims, preferred_element_type=F32, precision=precision)


def exact(a, b, nt=False):
    return dot(a, b, nt, lax.Precision.HIGHEST)


def quarters(x):
    h, w = x.shape[0] // 2, x.shape[1] // 2
    return (x[:h, :w] + x[:h, w:]) + (x[h:, :w] + x[h:, w:])


def product(x, y):
    return quarters(dot(x, y))


def kernel(
    ns, t_hbm, ops_hbm, env_hbm, assign_ref, parent_ref, out_ref, en_ref,
    t_ref, ops_ref, env_ref, in_sem,
    s_r, s_l, s_k, s_x, t_r, t_l, k_l, x_l, rt, lt,
    tc, lc, rc, ltc, rtc, m_u,
    up, rs_u, u_row, u_cand, xy_row, xy,
    dp, rs_d, d_row, d_cand, dd_row, dd,
    rs_e, e_row, e_cand, e_all, ss, rs,
):
    n = lax.axis_index("node")
    s = lax.axis_index("slab")
    b = env_ref.shape[0]
    w = b // ns
    rows = pl.ds(pl.multiple_of(s * w, w), w)
    leaf = n >= 8

    loads = [
        pltpu.make_async_copy(t_hbm, t_ref, in_sem.at[0]),
        pltpu.make_async_copy(ops_hbm, ops_ref, in_sem.at[1]),
        pltpu.make_async_copy(env_hbm, env_ref, in_sem.at[2]),
    ]
    for load in loads:
        load.start()

    def block(j):
        return pl.ds(pl.multiple_of(j * w, w), w)

    c0 = jnp.where(n >= 4, 8, jnp.where(n >= 2, 4, jnp.where(n >= 1, 2, 1)))
    c1 = jnp.where(n >= 8, 8, jnp.where(n >= 1, 2 * c0, 2))
    p0 = jnp.where(n >= 8, 4, jnp.where(n >= 4, 2, jnp.where(n >= 2, 1, 0)))
    p1 = jnp.where(n >= 2, 2 * p0, jnp.where(n >= 1, 1, 0))

    barrier = pltpu.get_barrier_semaphore()

    def greet_slab(k, c):
        pl.semaphore_signal(barrier, inc=1, device_id=(n, lax.rem(s + k, ns)), device_id_type=MESH)
        return c

    def greet_node(m, c):
        pl.semaphore_signal(barrier, inc=1, device_id=(m, s), device_id_type=MESH)
        return c

    lax.fori_loop(1, ns, greet_slab, 0)
    lax.fori_loop(p0, p1, greet_node, 0)

    @pl.when(n >= 2)
    def _():
        lax.fori_loop(c0, c1, greet_node, 0)

    @pl.when(n < 2)
    def _():
        def greet_all(k, c):
            m = c0 + k // ns
            pl.semaphore_signal(barrier, inc=1, device_id=(m, lax.rem(k, ns)), device_id_type=MESH)
            return c

        lax.fori_loop(0, (c1 - c0) * ns, greet_all, 0)

    @pl.when((n == 2) | (n == 3))
    def _():
        greet_node(5 - n, 0)

    pair_of_two = jnp.where((n == 2) | (n == 3), 1, 0)
    greetings = (ns - 1) + jnp.where((n >= 1) & (n < 4), ns, p1 - p0) + (c1 - c0) + pair_of_two

    def peer(k):
        return lax.rem(s + 1 + lax.rem(k + ns // 2 - 2, ns - 1), ns)

    def slab_copy(q, src, dst, to, frm):
        return pltpu.make_async_remote_copy(
            src_ref=src, dst_ref=dst, send_sem=ss.at[q, to], recv_sem=rs.at[q, frm],
            device_id=(n, to), device_id_type=MESH,
        )

    def slab_start(q, src_of, dst):
        def go(k, c):
            j = peer(k)
            slab_copy(q, src_of(j), dst, j, s).start()
            return c

        lax.fori_loop(1, ns, go, 0)

    def slab_wait(q, dst_of):
        def go(k, c):
            i = lax.rem(s + k, ns)
            slab_copy(q, dst_of(i), dst_of(i), i, i).wait_recv()
            return c

        lax.fori_loop(1, ns, go, 0)

    def slab_drain(q, src_of):
        def go(k, c):
            j = lax.rem(s + k, ns)
            slab_copy(q, src_of(j), src_of(j), j, s).wait_send()
            return c

        lax.fori_loop(1, ns, go, 0)

    def node_copy(q, src, dst, to, frm):
        return pltpu.make_async_remote_copy(
            src_ref=src, dst_ref=dst, send_sem=ss.at[q, to], recv_sem=rs.at[q, frm],
            device_id=(to, s), device_id_type=MESH,
        )

    def node_start(q, src, dst, lo, hi):
        def go(m, c):
            node_copy(q, src, dst, m, n).start()
            return c

        lax.fori_loop(lo, hi, go, 0)

    def node_wait(q, dst_of, lo, hi):
        def go(m, c):
            node_copy(q, dst_of(m), dst_of(m), m, m).wait_recv()
            return c

        lax.fori_loop(lo, hi, go, 0)

    def node_drain(q, src, lo, hi):
        def go(m, c):
            node_copy(q, src, src, m, n).wait_send()
            return c

        lax.fori_loop(lo, hi, go, 0)

    def spread(dst, i, x):
        dst.reshape(b * w, b)[pl.ds(i, b, stride=w), :] = x

    def a2a_start(q, src, dst):
        slab_start(q, lambda j: src.at[block(j)], dst.at[:, rows, :])
        dst[:, rows, :] = src[rows]

    def a2a_wait(q, dst):
        slab_wait(q, lambda i: dst.at[:, block(i), :])

    def a2a_drain(q, src):
        slab_drain(q, lambda j: src.at[block(j)])

    def part(i):
        return slice(i * b, (i + 1) * b)

    def sandwich(cat, turned, x, add=None):
        side = beside(x)
        weights = jnp.concatenate([side, side], axis=0)
        total = jnp.zeros((2 * b, 2 * b), F32)
        for i in range(0, w, 2):
            moved = []
            for k in (i, i + 1):
                both = dot(cat[part(k), :], weights)
                both = both[:, :b] + both[:, b:]
                if add is not None:
                    add[k] = add[k] + both
                moved.append(above(both))
            total = total + dot(jnp.concatenate(moved, axis=1), turned[i * b : (i + 2) * b, :])
        return quarters(total)

    def exact_sandwich(m, x):
        total = jnp.zeros((b, b), F32)
        for i in range(w):
            total = total + exact(exact(m[i], x), m[i], nt=True)
        return total

    def family(m):
        first = jnp.int32(NODES - 1)
        last = jnp.int32(0)
        for k in range(NODES - 1, 0, -1):
            first = jnp.where(parent_ref[k] == m, k, first)
        for k in range(1, NODES):
            last = jnp.where(parent_ref[k] == m, k, last)
        return first, last

    left_child, right_child = family(n)
    mine = parent_ref[n]
    eldest, _ = family(mine)
    side_of = jnp.where(eldest == n, 0, 1)
    first_id = assign_ref[0, n]
    second_id = assign_ref[1, n]

    loads[0].wait()

    @pl.when(n < 8)
    def _():
        for i in range(w):
            spread(s_r, i, t_ref[part(i), :].T)

    for i in range(w):
        spread(s_l, i, t_ref[part(i), :])
    pl.semaphore_wait(barrier, greetings)

    @pl.when(n < 8)
    def _():
        a2a_start(A2A_R, s_r, t_r)

    a2a_start(A2A_L, s_l, t_l)
    loads[1].wait()
    loads[2].wait()
    op_p = ops_ref[first_id]
    op_q = ops_ref[second_id]
    for i in range(w):
        t = t_ref[part(i), :]
        tq = exact(t, op_q)
        v = jnp.where(leaf, t + tq, tq)
        spread(s_k, i, exact(op_p, v) + jnp.where(leaf, tq, 0.0))
    a2a_start(A2A_K, s_k, k_l)

    def right_forms():
        a2a_wait(A2A_R, t_r)
        for i in range(w):
            x = t_r[i].T
            rt[i] = x
            rtc[part(i), :] = beside(x)
        for i in range(w):
            rc[part(i), :] = beside(t_r[i])

    def left_forms():
        a2a_wait(A2A_L, t_l)
        for i in range(w):
            x = t_l[i].T
            lt[i] = x
            ltc[part(i), :] = beside(x)
        for i in range(w):
            lc[part(i), :] = beside(t_l[i])

    def own_forms():
        for i in range(w):
            tc[part(i), :] = beside(t_ref[part(i), :])

    def pair_square():
        a2a_wait(A2A_K, k_l)
        total = jnp.zeros((b, b), F32)
        for i in range(w):
            total = total + exact(k_l[i], t_l[i], nt=True)
        up[...] = total

    def pick_d():
        node_wait(NODE_D, lambda m: d_cand.at[m], p0, p1)
        dd_row[...] = d_cand[mine, side_of]
        slab_start(AG_D, lambda j: dd_row, dd.at[rows, :])
        dd[rows, :] = dd_row[...]

    def gather_d():
        slab_wait(AG_D, lambda i: dd.at[block(i), :])

    def push_d():
        slab_start(RS_D, lambda j: dp.at[:, block(j), :], rs_d.at[s])
        rs_d[s] = dp[:, rows, :]

    def square_d():
        d = dd[...]
        dp[0] = sandwich(rtc, rc, d)
        dp[1] = sandwich(ltc, lc, d)
        push_d()

    def send_d():
        slab_wait(RS_D, lambda i: rs_d.at[i])
        total = rs_d[0]
        for k in range(1, ns):
            total = total + rs_d[k]
        d_row[...] = total
        node_start(NODE_D, d_row, d_cand.at[n], c0, c1)

    def push_u():
        slab_start(RS_U, lambda j: up.at[block(j), :], rs_u.at[s])
        rs_u[s] = up[rows, :]

    def send_u():
        slab_wait(RS_U, lambda i: rs_u.at[i])
        total = rs_u[0]
        for k in range(1, ns):
            total = total + rs_u[k]
        u_row[...] = total
        node_start(NODE_U, u_row, u_cand.at[n], p0, p1)

    def spread_u():
        slab_start(AG_U, lambda j: xy_row, xy.at[:, rows, :])
        xy[:, rows, :] = xy_row[...]

    def pick_u():
        node_wait(NODE_U, lambda m: u_cand.at[m], c0, c1)
        xy_row[0] = u_cand[left_child]
        xy_row[1] = u_cand[right_child]
        spread_u()

    def merged_copy(src, slot, owner, to, frm):
        return pltpu.make_async_remote_copy(
            src_ref=src, dst_ref=m_u.at[slot, frm], send_sem=ss.at[MERGE, owner], recv_sem=rs.at[MERGE + slot, frm],
            device_id=(to, owner), device_id_type=MESH,
        )

    def push_merged():
        def go(k, c):
            j = lax.rem(s + k + ns // 2, ns)
            merged_copy(up.at[block(j), :], jnp.where(n == 3, 1, 0), j, n // 2, s).start()
            return c

        lax.fori_loop(0, ns, go, 0)

    def drain_merged():
        def go(j, c):
            merged_copy(up.at[block(j), :], 0, j, n // 2, s).wait_send()
            return c

        lax.fori_loop(0, ns, go, 0)

    def pick_merged(slot):
        def go(i, c):
            merged_copy(m_u.at[slot, i], slot, i, n, i).wait_recv()
            return c

        lax.fori_loop(0, ns, go, 0)
        total = m_u[slot, 0]
        for k in range(1, ns):
            total = total + m_u[slot, k]
        xy_row[slot] = total

    def gather_u():
        slab_wait(AG_U, lambda i: xy.at[:, block(i), :])

    def square_u():
        up[...] = up[...] + (sandwich(rc, rtc, xy[0]) + sandwich(lc, ltc, xy[1], add=k_l))

    def move_left():
        x = above(xy[0])
        for i in range(w):
            spread(s_x, i, product(x, tc[part(i), :]))
        a2a_start(A2A_X, s_x, x_l)

    def push_energy(square):
        terms = dd[...] * square
        total = terms[0:w, :]
        for k in range(1, ns):
            total = total + terms[k * w : (k + 1) * w, :]
        rs_e[s] = total
        slab_start(SLAB_E, lambda j: rs_e.at[s], rs_e.at[s])

    def own_energy():
        slab_wait(SLAB_E, lambda i: rs_e.at[i])
        total = rs_e[0]
        for k in range(1, ns):
            total = total + rs_e[k]
        return total

    def wait_total(frm):
        node_wait(NODE_F, lambda m: e_all, frm, frm + 1)

    def drain_first():
        a2a_drain(A2A_L, s_l)
        a2a_drain(A2A_K, s_k)

        @pl.when(n < 8)
        def _():
            a2a_drain(A2A_R, s_r)

    factor = b**0.75

    @pl.when(leaf)
    def _():
        a2a_wait(A2A_L, t_l)
        pair_square()
        push_u()
        send_u()
        drain_first()
        pick_d()
        gather_d()

    @pl.when((n >= 4) & (n < 8))
    def _():
        right_forms()
        left_forms()
        pair_square()
        own_forms()
        pick_u()
        gather_u()
        square_u()
        push_u()
        send_u()
        move_left()
        drain_first()
        pick_d()
        gather_d()
        square_d()
        send_d()
        wait_total(2)
        node_start(NODE_F, e_all, e_all, 2 * n, 2 * n + 2)

    @pl.when((n == 2) | (n == 3))
    def _():
        right_forms()
        left_forms()
        pair_square()
        own_forms()
        drain_first()
        pick_d()
        gather_d()
        square_d()
        pick_u()
        send_d()
        gather_u()
        square_u()
        push_merged()
        push_energy(up[...])
        move_left()
        e_row[...] = own_energy()
        e_cand[n] = e_row[...]
        node_start(NODE_E, e_row, e_cand.at[n], 5 - n, 6 - n)
        node_wait(NODE_E, lambda m: e_cand.at[m], 1, 2)
        node_wait(NODE_E, lambda m: e_cand.at[m], 5 - n, 6 - n)
        e_all[...] = e_cand[1] + (e_cand[2] + e_cand[3])

        @pl.when(n == 2)
        def _():
            node_start(NODE_F, e_all, e_all, 4, 8)
            node_start(NODE_F, e_all, e_all, 1, 2)

    @pl.when(n == 1)
    def _():
        right_forms()
        left_forms()
        pick_d()
        gather_d()
        d = dd[...]
        dp[0] = exact_sandwich(rt, d)
        dp[1] = exact_sandwich(lt, d)
        push_d()
        send_d()
        pair_square()
        push_energy(up[...])
        own_forms()
        own = own_energy()
        node_wait(NODE_E, lambda m: e_cand.at[m], 0, 1)
        e_row[...] = own + e_cand[0]
        node_start(NODE_E, e_row, e_cand.at[n], 2, 4)
        drain_first()
        pick_merged(0)
        pick_merged(1)
        spread_u()
        gather_u()
        square_u()
        push_merged()
        move_left()
        wait_total(2)
        node_start(NODE_F, e_all, e_all, 0, 1)

    @pl.when(n == 0)
    def _():
        dd[...] = env_ref[...]
        right_forms()
        dp[0] = exact_sandwich(rt, env_ref[...])
        dp[1] = jnp.zeros((b, b), F32)
        push_d()
        send_d()
        left_forms()
        d = above(env_ref[...] * factor)
        for i in range(w):
            x_l[i] = product(d, lc[part(i), :])
        slab_start(A2A_Z, lambda j: x_l.at[:, block(j), :], s_x.at[rows])
        s_x[rows] = x_l[:, rows, :]
        pair_square()
        push_energy(up[...] + sandwich(lc, ltc, op_q))
        e_row[...] = own_energy()
        node_start(NODE_E, e_row, e_cand.at[n], 1, 2)
        slab_wait(A2A_Z, lambda i: s_x.at[block(i)])
        q_side = beside(op_q)
        q_weights = jnp.concatenate([q_side, q_side], axis=0)
        p_above = above(op_p)
        for i in range(w):
            side = beside(s_x.reshape(b * w, b)[pl.ds(i, b, stride=w), :])
            tc[part(i), :] = side
            moved = dot(side, q_weights)
            moved = moved[:, :b] + moved[:, b:]
            t_r[i] = product(p_above, beside(moved)) + moved
        drain_first()
        slab_drain(A2A_Z, lambda j: x_l.at[:, block(j), :])
        slab_drain(RS_D, lambda j: dp.at[:, block(j), :])
        node_drain(NODE_D, d_row, c0, c1)
        slab_drain(SLAB_E, lambda j: rs_e.at[s])
        node_drain(NODE_E, e_row, 1, 2)
        pick_merged(0)
        slab_start(AG_U, lambda j: xy_row.at[0], xy.at[0, rows, :])
        xy[0, rows, :] = xy_row[0]
        slab_wait(AG_U, lambda i: xy.at[0, block(i), :])
        x = above(xy[0])
        for i in range(w):
            k_l[i] = product(x, tc[part(i), :]) + t_r[i]
        slab_start(A2A_X, lambda j: k_l.at[:, block(j), :], out_ref.at[rows])
        out_ref[rows] = k_l[:, rows, :]
        wait_total(1)
        slab_drain(AG_U, lambda j: xy_row.at[0])
        slab_wait(A2A_X, lambda i: out_ref.at[block(i)])
        slab_drain(A2A_X, lambda j: k_l.at[:, block(j), :])

    @pl.when(n >= 1)
    def _():
        @pl.when(n < 8)
        def _():
            a2a_wait(A2A_X, x_l)

        d = above(dd[...] * factor)
        for i in range(w):
            side = beside(k_l[i] + jnp.where(n < 8, x_l[i], 0.0))
            out_ref.reshape(b * w, b)[pl.ds(i, b, stride=w), :] = product(d, side)

    @pl.when(leaf)
    def _():
        wait_total(n // 2)

    en_ref[...] = jnp.sum(e_all[...], axis=(0, 1), keepdims=True)

    @pl.when((n >= 1) & (n < 8))
    def _():
        a2a_drain(A2A_X, s_x)
        slab_drain(RS_D, lambda j: dp.at[:, block(j), :])
        node_drain(NODE_D, d_row, c0, c1)
        slab_drain(AG_U, lambda j: xy_row)

    @pl.when(n >= 1)
    def _():
        slab_drain(AG_D, lambda j: dd_row)

    @pl.when(n >= 4)
    def _():
        slab_drain(RS_U, lambda j: up.at[block(j), :])
        node_drain(NODE_U, u_row, p0, p1)

    @pl.when((n >= 1) & (n < 4))
    def _():
        drain_merged()
        slab_drain(SLAB_E, lambda j: rs_e.at[s])
        node_drain(NODE_E, e_row, jnp.where(n >= 2, 5 - n, n + 1), jnp.where(n >= 2, 6 - n, 2 * n + 2))

    @pl.when(n == 1)
    def _():
        node_drain(NODE_F, e_all, 0, 1)

    @pl.when(n == 2)
    def _():
        node_drain(NODE_F, e_all, 4, 8)
        node_drain(NODE_F, e_all, 1, 2)

    @pl.when((n >= 4) & (n < 8))
    def _():
        node_drain(NODE_F, e_all, 2 * n, 2 * n + 2)


def per_device(ns, tensors, ops, assign, parent, env):
    b = env.shape[0]
    w = b // ns
    stack = pltpu.VMEM((w * b, b), F32)
    full = pltpu.VMEM((b, w, b), F32)
    form = pltpu.VMEM((w, b, b), F32)
    cat = pltpu.VMEM((w * b, 2 * b), BF16)
    square = pltpu.VMEM((b, b), F32)
    slab = pltpu.VMEM((w, b), F32)
    two = pltpu.VMEM((2, w, b), F32)
    slots = max(ns, NODES)
    smem = pl.BlockSpec(memory_space=pltpu.SMEM)
    hbm = pl.BlockSpec(memory_space=pl.ANY)
    vmem = pl.BlockSpec(memory_space=pltpu.VMEM)
    grad, energy = pl.pallas_call(
        functools.partial(kernel, ns),
        out_shape=(pltpu.VMEM((b, w, b), F32), jax.ShapeDtypeStruct((1, 1), F32)),
        in_specs=[hbm, hbm, hbm, smem, smem],
        out_specs=(vmem, vmem),
        scratch_shapes=[
            stack, pltpu.VMEM(ops.shape, F32), square, pltpu.SemaphoreType.DMA((3,)),
            full, full, full, full, form, form, form, form, form, form,
            cat, cat, cat, cat, cat, pltpu.VMEM((2, ns, w, b), F32),
            square, pltpu.VMEM((ns, w, b), F32), slab, pltpu.VMEM((NODES, w, b), F32), two, pltpu.VMEM((2, b, b), F32),
            pltpu.VMEM((2, b, b), F32), pltpu.VMEM((ns, 2, w, b), F32), two,
            pltpu.VMEM((NODES, 2, w, b), F32), slab, square,
            pltpu.VMEM((ns, w, b), F32), slab, pltpu.VMEM((NODES, w, b), F32), slab,
            pltpu.SemaphoreType.DMA((16, slots)), pltpu.SemaphoreType.DMA((16, slots)),
        ],
        compiler_params=pltpu.CompilerParams(collective_id=0, has_side_effects=True),
    )(tensors.reshape(w * b, b), ops, env, assign.T, parent)
    return grad[None], energy[0, 0]


def solution(mesh):
    return jax.shard_map(
        functools.partial(per_device, mesh.shape["slab"]),
        mesh=mesh,
        in_specs=(P("node", "slab", None, None), P(), P(), P(), P()),
        out_specs=(P("node", None, "slab", None), P()),
        check_vma=False,
    )
```

```python
import functools

import jax
import jax.numpy as jnp
from jax import lax
from jax.experimental import pallas as pl
from jax.experimental.pallas import tpu as pltpu
from jax.sharding import PartitionSpec as P

NODES = 16
MESH = pl.DeviceIdType.MESH
F32 = jnp.float32
BF16 = jnp.bfloat16

A2A_R, A2A_L, A2A_K, A2A_X, RS_U, RS_D, AG_U, AG_D, SLAB_E, NODE_U, NODE_D, NODE_E, NODE_F, A2A_Z, MERGE, MERGE2, COPIES, COUNT = range(18)


def split(x):
    hi = x.astype(BF16)
    return hi, (x - hi.astype(F32)).astype(BF16)


def beside(x):
    return jnp.concatenate(split(x), axis=1)


def above(x):
    return jnp.concatenate(split(x), axis=0)


def dot(a, b, nt=False, precision=None):
    dims = (((1,), (1 if nt else 0,)), ((), ()))
    return lax.dot_general(a, b, dims, preferred_element_type=F32, precision=precision)


def exact(a, b, nt=False):
    return dot(a, b, nt, lax.Precision.HIGHEST)


def quarters(x):
    h, w = x.shape[0] // 2, x.shape[1] // 2
    return (x[:h, :w] + x[:h, w:]) + (x[h:, :w] + x[h:, w:])


def product(x, y):
    return quarters(dot(x, y))


def kernel(
    ns, t_hbm, ops_hbm, env_hbm, assign_hbm, parent_hbm, out_ref, en_ref,
    t_ref, ops_ref, env_ref, assign_ref, parent_ref, in_sem,
    s_r, s_l, s_k, s_x, t_r, t_l, k_l, x_l, rt, lt,
    tc, lc, rc, ltc, rtc, m_u,
    up, rs_u, u_row, u_cand, xy_row, xy,
    dp, rs_d, d_row, d_cand, dd_row, dd,
    rs_e, e_row, e_cand, e_all, z, zc, base, gb, x_near, p_one, ss, rs,
):
    n = lax.axis_index("node")
    s = lax.axis_index("slab")
    b = env_ref.shape[0]
    w = b // ns
    rows = pl.ds(pl.multiple_of(s * w, w), w)
    leaf = n >= 8

    loads = [
        pltpu.make_async_copy(t_hbm, t_ref, in_sem.at[0]),
        pltpu.make_async_copy(ops_hbm, ops_ref, in_sem.at[1]),
        pltpu.make_async_copy(env_hbm, env_ref, in_sem.at[2]),
        pltpu.make_async_copy(assign_hbm, assign_ref, in_sem.at[3]),
        pltpu.make_async_copy(parent_hbm, parent_ref, in_sem.at[4]),
    ]
    for load in (loads[0], loads[3], loads[4]):
        load.start()

    def block(j):
        return pl.ds(pl.multiple_of(j * w, w), w)

    c0 = jnp.where(n >= 4, 8, jnp.where(n >= 2, 4, jnp.where(n >= 1, 2, 1)))
    c1 = jnp.where(n >= 8, 8, jnp.where(n >= 1, 2 * c0, 2))
    p0 = jnp.where(n >= 8, 4, jnp.where(n >= 4, 2, jnp.where(n >= 2, 1, 0)))
    p1 = jnp.where(n >= 2, 2 * p0, jnp.where(n >= 1, 1, 0))

    barrier = pltpu.get_barrier_semaphore()

    def greet_slab(k, c):
        pl.semaphore_signal(barrier, inc=1, device_id=(n, lax.rem(s + k, ns)), device_id_type=MESH)
        return c

    def greet_node(m, c):
        pl.semaphore_signal(barrier, inc=1, device_id=(m, s), device_id_type=MESH)
        return c

    lax.fori_loop(1, ns, greet_slab, 0)
    lax.fori_loop(p0, p1, greet_node, 0)

    @pl.when(n >= 2)
    def _():
        lax.fori_loop(c0, c1, greet_node, 0)

    @pl.when(n < 2)
    def _():
        def greet_all(k, c):
            m = c0 + k // ns
            pl.semaphore_signal(barrier, inc=1, device_id=(m, lax.rem(k, ns)), device_id_type=MESH)
            return c

        lax.fori_loop(0, (c1 - c0) * ns, greet_all, 0)

    @pl.when((n == 2) | (n == 3))
    def _():
        greet_node(5 - n, 0)

    pair_of_two = jnp.where((n == 2) | (n == 3), 1, 0)
    greetings = (ns - 1) + jnp.where((n >= 1) & (n < 4), ns, p1 - p0) + (c1 - c0) + pair_of_two

    def peer(k):
        return lax.rem(s + 1 + lax.rem(k + ns // 2 - 2, ns - 1), ns)

    def remote(q, src, dst, to, slab, arrival=None):
        return pltpu.make_async_remote_copy(
            src_ref=src, dst_ref=dst, send_sem=ss.at[q], recv_sem=rs.at[q if arrival is None else arrival],
            device_id=(to, slab), device_id_type=MESH,
        )

    def arrived(q, like):
        remote(q, like, like, n, lax.rem(s + 1, ns)).wait_recv()

    def drained(q, like):
        remote(q, like, like, n, lax.rem(s + 1, ns)).wait_send()

    def slab_start(q, src_of, dst):
        def go(k, c):
            j = peer(k)
            remote(q, src_of(j), dst, n, j).start()
            return c

        lax.fori_loop(1, ns, go, 0)

    def node_start(q, src, dst, lo, hi):
        def go(m, c):
            remote(q, src, dst, m, s).start()
            return c

        lax.fori_loop(lo, hi, go, 0)

    others = pl.ds(0, ns - 1)
    other_rows = pl.ds(0, b - w)

    def spread(dst, i, x):
        dst.reshape(b * w, b)[pl.ds(i, b, stride=w), :] = x

    def a2a_start(q, src, dst):
        slab_start(q, lambda j: src.at[block(j)], dst.at[:, rows, :])
        dst[:, rows, :] = src[rows]

    def a2a_wait(q, dst):
        arrived(q, dst.at[:, other_rows, :])

    def a2a_drain(q, src):
        drained(q, src.at[other_rows])

    def part(i):
        return slice(i * b, (i + 1) * b)

    def sandwich(cat, turned, x, add=None):
        side = beside(x)
        weights = jnp.concatenate([side, side], axis=0)
        total = jnp.zeros((2 * b, 2 * b), F32)
        for i in range(0, w, 2):
            moved = []
            for k in (i, i + 1):
                both = dot(cat[part(k), :], weights)
                both = both[:, :b] + both[:, b:]
                if add is not None:
                    add[k] = add[k] + both
                moved.append(above(both))
            total = total + dot(jnp.concatenate(moved, axis=1), turned[i * b : (i + 2) * b, :])
        return quarters(total)

    def exact_sandwich(m, x):
        total = jnp.zeros((b, b), F32)
        for i in range(w):
            total = total + exact(exact(m[i], x), m[i], nt=True)
        return total

    def family(m):
        first = jnp.int32(NODES - 1)
        last = jnp.int32(0)
        for k in range(NODES - 1, 0, -1):
            first = jnp.where(parent_ref[k] == m, k, first)
        for k in range(1, NODES):
            last = jnp.where(parent_ref[k] == m, k, last)
        return first, last

    loads[0].wait()
    loads[1].start()
    loads[2].start()

    @pl.when(n < 8)
    def _():
        for i in range(w):
            spread(s_r, i, t_ref[part(i), :].T)

    for i in range(w):
        spread(s_l, i, t_ref[part(i), :])
    pl.semaphore_wait(barrier, greetings)

    @pl.when(n < 8)
    def _():
        a2a_start(A2A_R, s_r, t_r)

    a2a_start(A2A_L, s_l, t_l)
    for load in loads[1:]:
        load.wait()
    left_child, right_child = family(n)
    mine = parent_ref[n]
    eldest, _ = family(mine)
    side_of = jnp.where(eldest == n, 0, 1)
    first_id = assign_ref[0, n]
    second_id = assign_ref[1, n]
    op_p = ops_ref[first_id]
    op_q = ops_ref[second_id]
    for i in range(w):
        t = t_ref[part(i), :]
        tq = exact(t, op_q)
        v = jnp.where(leaf, t + tq, tq)
        spread(s_k, i, exact(op_p, v) + jnp.where(leaf, tq, 0.0))
    a2a_start(A2A_K, s_k, k_l)

    def right_forms():
        a2a_wait(A2A_R, t_r)
        for i in range(w):
            x = t_r[i].T
            rt[i] = x
            rtc[part(i), :] = beside(x)
        for i in range(w):
            rc[part(i), :] = beside(t_r[i])

    def left_forms():
        a2a_wait(A2A_L, t_l)
        for i in range(w):
            x = t_l[i].T
            lt[i] = x
            ltc[part(i), :] = beside(x)
        for i in range(w):
            lc[part(i), :] = beside(t_l[i])

    def own_forms():
        for i in range(w):
            tc[part(i), :] = beside(t_ref[part(i), :])

    def pair_square():
        a2a_wait(A2A_K, k_l)
        total = jnp.zeros((b, b), F32)
        for i in range(w):
            total = total + exact(k_l[i], t_l[i], nt=True)
        up[...] = total

    def pick_d(count):
        arrived(NODE_D, d_cand.at[pl.ds(0, count)])
        dd_row[...] = d_cand[mine, side_of]
        slab_start(AG_D, lambda j: dd_row, dd.at[rows, :])
        dd[rows, :] = dd_row[...]

    def gather_d():
        arrived(AG_D, dd.at[other_rows, :])

    def push_d():
        slab_start(RS_D, lambda j: dp.at[:, block(j), :], rs_d.at[s])
        rs_d[s] = dp[:, rows, :]

    def square_d():
        d = dd[...]
        dp[0] = sandwich(rtc, rc, d)
        dp[1] = sandwich(ltc, lc, d)
        push_d()

    def send_d():
        arrived(RS_D, rs_d.at[others])
        total = rs_d[0]
        for k in range(1, ns):
            total = total + rs_d[k]
        d_row[...] = total
        node_start(NODE_D, d_row, d_cand.at[n], c0, c1)

    def push_u():
        slab_start(RS_U, lambda j: up.at[block(j), :], rs_u.at[s])
        rs_u[s] = up[rows, :]

    def send_u():
        arrived(RS_U, rs_u.at[others])
        total = rs_u[0]
        for k in range(1, ns):
            total = total + rs_u[k]
        u_row[...] = total
        node_start(NODE_U, u_row, u_cand.at[n], p0, p1)

    def spread_u():
        slab_start(AG_U, lambda j: xy_row, xy.at[:, rows, :])
        xy[:, rows, :] = xy_row[...]

    def pick_u(count):
        arrived(NODE_U, u_cand.at[pl.ds(0, count)])
        xy_row[0] = u_cand[left_child]
        xy_row[1] = u_cand[right_child]
        spread_u()

    def push_merged():
        slot = jnp.where(n == 3, 1, 0)

        def go(k, c):
            j = lax.rem(s + k + ns // 2, ns)
            remote(MERGE, up.at[block(j), :], m_u.at[slot, s], n // 2, j, MERGE + slot).start()
            return c

        lax.fori_loop(0, ns, go, 0)

    def pick_merged(slot):
        arrived(MERGE + slot, m_u.at[slot])
        total = m_u[slot, 0]
        for k in range(1, ns):
            total = total + m_u[slot, k]
        xy_row[slot] = total

    def gather_u():
        arrived(AG_U, xy.at[:, other_rows, :])

    def square_u():
        up[...] = up[...] + (sandwich(rc, rtc, xy[0]) + sandwich(lc, ltc, xy[1], add=k_l))

    def move_left():
        x = above(xy[0])
        for i in range(w):
            spread(s_x, i, product(x, tc[part(i), :]))
        a2a_start(A2A_X, s_x, x_l)

    def push_energy(square):
        terms = dd[...] * square
        total = terms[0:w, :]
        for k in range(1, ns):
            total = total + terms[k * w : (k + 1) * w, :]
        rs_e[s] = total
        slab_start(SLAB_E, lambda j: rs_e.at[s], rs_e.at[s])

    def own_energy():
        arrived(SLAB_E, rs_e.at[others])
        total = rs_e[0]
        for k in range(1, ns):
            total = total + rs_e[k]
        return total

    def wait_total():
        arrived(NODE_F, e_all)

    def drain_first():
        a2a_drain(A2A_L, s_l)
        a2a_drain(A2A_K, s_k)

        @pl.when(n < 8)
        def _():
            a2a_drain(A2A_R, s_r)

    factor = b**0.75

    @pl.when(leaf)
    def _():
        a2a_wait(A2A_L, t_l)
        pair_square()
        push_u()
        send_u()
        drain_first()
        pick_d(4)
        gather_d()

    @pl.when((n >= 4) & (n < 8))
    def _():
        right_forms()
        left_forms()
        pair_square()
        own_forms()
        pick_u(8)
        gather_u()
        square_u()
        push_u()
        send_u()
        move_left()
        drain_first()
        pick_d(2)
        gather_d()
        square_d()
        send_d()
        wait_total()
        node_start(NODE_F, e_all, e_all, 2 * n, 2 * n + 2)

    @pl.when((n == 2) | (n == 3))
    def _():
        right_forms()
        left_forms()
        pair_square()
        own_forms()
        drain_first()
        pick_d(1)
        gather_d()
        square_d()
        pick_u(4)
        send_d()
        gather_u()
        square_u()
        push_merged()
        push_energy(up[...])
        move_left()
        e_row[...] = own_energy()
        e_cand[n] = e_row[...]
        node_start(NODE_E, e_row, e_cand.at[n], 5 - n, 6 - n)
        arrived(NODE_E, e_cand.at[pl.ds(0, 2)])
        e_all[...] = e_cand[1] + (e_cand[2] + e_cand[3])

        @pl.when(n == 2)
        def _():
            node_start(NODE_F, e_all, e_all, 4, 8)
            node_start(NODE_F, e_all, e_all, 1, 2)

    @pl.when(n == 1)
    def _():
        right_forms()
        left_forms()
        pick_d(1)
        gather_d()
        d = dd[...]
        dp[0] = exact_sandwich(rt, d)
        dp[1] = exact_sandwich(lt, d)
        push_d()
        send_d()
        pair_square()
        push_energy(up[...])
        own_forms()
        own = own_energy()
        arrived(NODE_E, e_cand.at[0])
        e_row[...] = own + e_cand[0]
        node_start(NODE_E, e_row, e_cand.at[n], 2, 4)
        drain_first()
        pick_merged(0)
        pick_merged(1)
        spread_u()
        gather_u()
        square_u()
        push_merged()
        move_left()
        wait_total()
        node_start(NODE_F, e_all, e_all, 0, 1)

    @pl.when(n == 0)
    def _():
        chips = ns // 2
        chip, core = s // 2, lax.rem(s, 2)
        near = [chip, lax.rem(chip + 2, chips), lax.rem(chip + chips - 2, chips)]
        z_peer = s + 2 - 4 * lax.rem(chip, 2)
        holders = [s, z_peer, lax.rem(s + chips, ns), lax.rem(z_peer + chips, ns)]
        kept = len(holders)

        dd[...] = env_ref[...]
        right_forms()
        dp[0] = exact_sandwich(rt, env_ref[...])
        dp[1] = jnp.zeros((b, b), F32)
        push_d()
        send_d()
        left_forms()
        d = above(env_ref[...] * factor)
        for i in range(w):
            x_l[i] = product(d, lc[part(i), :])
        slab_start(A2A_Z, lambda j: x_l.at[:, block(j), :], z.at[0, rows])
        z[0, rows] = x_l[:, rows, :]
        pair_square()
        push_energy(up[...] + sandwich(lc, ltc, op_q))
        e_row[...] = own_energy()
        node_start(NODE_E, e_row, e_cand.at[n], 1, 2)
        arrived(A2A_Z, z.at[0, other_rows])
        for k in range(1, kept):
            remote(COPIES, z.at[0], z.at[k], n, holders[k]).start()
        q_side = beside(op_q)
        q_weights = jnp.concatenate([q_side, q_side], axis=0)
        same = lax.broadcasted_iota(jnp.int32, (b, b), 0) == lax.broadcasted_iota(jnp.int32, (b, b), 1)
        p_one[...] = op_p + jnp.where(same, 1.0, 0.0)

        def chip_rows(m):
            return pl.ds(pl.multiple_of(m * (2 * w), 2 * w), 2 * w)

        p_near = above(jnp.concatenate([p_one[chip_rows(m), :] for m in near], axis=0))
        drain_first()
        drained(A2A_Z, x_l.at[:, other_rows, :])
        drained(RS_D, dp.at[:, other_rows, :])
        drained(NODE_D, d_row)
        drained(SLAB_E, rs_e.at[others])
        drained(NODE_E, e_row)
        arrived(COPIES, z.at[pl.ds(1, kept - 1)])
        drained(COPIES, z.at[pl.ds(1, kept - 1)])

        def known(q, c):
            side = beside(z.reshape(kept * b * w, b)[pl.ds((q // w) * (b * w) + lax.rem(q, w), b, stride=w), :])
            zc[q] = side
            moved = dot(side, q_weights)
            base[q] = product(p_near, beside(moved[:, :b] + moved[:, b:]))
            return c

        lax.fori_loop(0, kept * w, known, 0)

        pick_merged(0)
        mine_at = pl.ds(pl.multiple_of(core * w, w), w)
        ahead_at = pl.ds(pl.multiple_of((core + 4) * w, w), w)
        behind_at = pl.ds(pl.multiple_of((core + 2) * w, w), w)
        for c in range(2):
            remote(AG_U, xy_row.at[0], x_near.at[ahead_at, :], n, 2 * near[1] + c).start()
            remote(AG_U, xy_row.at[0], x_near.at[behind_at, :], n, 2 * near[2] + c).start()
        remote(AG_U, xy_row.at[0], x_near.at[mine_at, :], n, s + 1 - 2 * core).start()
        x_near[mine_at, :] = xy_row[0]
        arrived(AG_U, x_near.at[pl.ds(0, 5 * w), :])
        x = above(x_near[...])
        x_own = above(x_near[0 : 2 * w, :])

        def span(m):
            return pl.ds(pl.multiple_of(m * w, w), w)

        for k in range(kept):
            count = 6 if k < 2 else 2
            for i in range(w):
                q = k * w + i
                g = product(x if k < 2 else x_own, zc[q]) + base[q, 0 : count * w, :]
                for t in range(count):
                    gb[t, q] = g[t * w : (t + 1) * w, :]
            for t in range(2, count):
                remote(A2A_X, gb.at[t, pl.ds(k * w, w)], out_ref.at[span(holders[k])], n, 2 * near[t // 2] + t % 2).start()
        for k in range(kept):
            remote(A2A_X, gb.at[1 - core, pl.ds(k * w, w)], out_ref.at[span(holders[k])], n, s + 1 - 2 * core).start()
            out_ref[span(holders[k])] = gb[core, pl.ds(k * w, w)]
        wait_total()
        drained(AG_U, x_near.at[pl.ds(0, 5 * w), :])
        arrived(A2A_X, out_ref.at[pl.ds(0, 12 * w)])
        drained(A2A_X, out_ref.at[pl.ds(0, 12 * w)])

    @pl.when(n >= 1)
    def _():
        @pl.when(n < 8)
        def _():
            a2a_wait(A2A_X, x_l)

        d = above(dd[...] * factor)
        for i in range(w):
            side = beside(k_l[i] + jnp.where(n < 8, x_l[i], 0.0))
            out_ref.reshape(b * w, b)[pl.ds(i, b, stride=w), :] = product(d, side)

    @pl.when(leaf)
    def _():
        wait_total()

    en_ref[...] = jnp.sum(e_all[...], axis=(0, 1), keepdims=True)

    @pl.when((n >= 1) & (n < 8))
    def _():
        a2a_drain(A2A_X, s_x)
        drained(RS_D, dp.at[:, other_rows, :])
        drained(AG_U, xy.at[:, other_rows, :])

    @pl.when(n >= 1)
    def _():
        drained(AG_D, dd.at[other_rows, :])

    @pl.when(n >= 4)
    def _():
        drained(RS_U, up.at[other_rows, :])

    @pl.when((n >= 1) & (n < 4))
    def _():
        drained(MERGE, up)
        drained(SLAB_E, rs_e.at[others])

    @pl.when(n == 1)
    def _():
        drained(NODE_D, d_cand.at[pl.ds(0, 2)])
        drained(NODE_E, e_cand.at[pl.ds(0, 2)])
        drained(NODE_F, e_all)

    @pl.when((n == 2) | (n == 3))
    def _():
        drained(NODE_D, d_cand.at[pl.ds(0, 4)])
        drained(NODE_E, e_row)

    @pl.when(n == 2)
    def _():
        drained(NODE_F, e_cand.at[pl.ds(0, 5)])

    @pl.when((n >= 4) & (n < 8))
    def _():
        drained(NODE_D, d_cand.at[pl.ds(0, 8)])
        drained(NODE_U, u_cand.at[pl.ds(0, 2)])
        drained(NODE_F, e_cand.at[pl.ds(0, 2)])

    @pl.when(leaf)
    def _():
        drained(NODE_U, u_cand.at[pl.ds(0, 4)])


def per_device(ns, tensors, ops, assign, parent, env):
    b = env.shape[0]
    w = b // ns
    stack = pltpu.VMEM((w * b, b), F32)
    full = pltpu.VMEM((b, w, b), F32)
    form = pltpu.VMEM((w, b, b), F32)
    cat = pltpu.VMEM((w * b, 2 * b), BF16)
    square = pltpu.VMEM((b, b), F32)
    slab = pltpu.VMEM((w, b), F32)
    two = pltpu.VMEM((2, w, b), F32)
    hbm = pl.BlockSpec(memory_space=pl.ANY)
    vmem = pl.BlockSpec(memory_space=pltpu.VMEM)
    grad, energy = pl.pallas_call(
        functools.partial(kernel, ns),
        out_shape=(pltpu.VMEM((b, w, b), F32), jax.ShapeDtypeStruct((1, 1), F32)),
        in_specs=[hbm] * 5,
        out_specs=(vmem, vmem),
        scratch_shapes=[
            stack, pltpu.VMEM(ops.shape, F32), square,
            pltpu.SMEM((2, NODES), jnp.int32), pltpu.SMEM((NODES,), jnp.int32), pltpu.SemaphoreType.DMA((5,)),
            full, full, full, full, form, form, form, form, form, form,
            cat, cat, cat, cat, cat, pltpu.VMEM((2, ns, w, b), F32),
            square, pltpu.VMEM((ns, w, b), F32), slab, pltpu.VMEM((NODES, w, b), F32), two, pltpu.VMEM((2, b, b), F32),
            pltpu.VMEM((2, b, b), F32), pltpu.VMEM((ns, 2, w, b), F32), two,
            pltpu.VMEM((NODES, 2, w, b), F32), slab, square,
            pltpu.VMEM((ns, w, b), F32), slab, pltpu.VMEM((NODES, w, b), F32), slab,
            pltpu.VMEM((4, b, w, b), F32), pltpu.VMEM((4 * w, b, 2 * b), BF16), pltpu.VMEM((4 * w, 6 * w, b), F32),
            pltpu.VMEM((6, 4 * w, w, b), F32), pltpu.VMEM((6 * w, b), F32), square,
            pltpu.SemaphoreType.DMA((COUNT,)), pltpu.SemaphoreType.DMA((COUNT,)),
        ],
        compiler_params=pltpu.CompilerParams(collective_id=0, has_side_effects=True),
    )(tensors.reshape(w * b, b), ops, env, assign.T, parent)
    return grad[None], energy[0, 0]


def solution(mesh):
    return jax.shard_map(
        functools.partial(per_device, mesh.shape["slab"]),
        mesh=mesh,
        in_specs=(P("node", "slab", None, None), P(), P(), P(), P()),
        out_specs=(P("node", None, "slab", None), P()),
        check_vma=False,
    )
```

```python
import functools

import jax
import jax.numpy as jnp
from jax import lax
from jax.experimental import pallas as pl
from jax.experimental.pallas import tpu as pltpu
from jax.sharding import PartitionSpec as P

NODES = 16
MESH = pl.DeviceIdType.MESH
F32 = jnp.float32
BF16 = jnp.bfloat16

A2A_R, A2A_L, A2A_K, A2A_X, RS_U, RS_D, AG_U, AG_D, SLAB_E, NODE_U, NODE_D, NODE_E, NODE_F, A2A_Z, MERGE, MERGE2, COPIES, COUNT = range(18)


def split(x):
    hi = x.astype(BF16)
    return hi, (x - hi.astype(F32)).astype(BF16)


def beside(x):
    return jnp.concatenate(split(x), axis=1)


def above(x):
    return jnp.concatenate(split(x), axis=0)


def dot(a, b, nt=False, precision=None):
    dims = (((1,), (1 if nt else 0,)), ((), ()))
    return lax.dot_general(a, b, dims, preferred_element_type=F32, precision=precision)


def exact(a, b, nt=False):
    return dot(a, b, nt, lax.Precision.HIGHEST)


def quarters(x):
    h, w = x.shape[0] // 2, x.shape[1] // 2
    return (x[:h, :w] + x[:h, w:]) + (x[h:, :w] + x[h:, w:])


def product(x, y):
    return quarters(dot(x, y))


def kernel(
    ns, t_hbm, ops_hbm, env_hbm, assign_hbm, parent_hbm, out_ref, en_ref,
    t_ref, ops_ref, env_ref, assign_ref, parent_ref, in_sem,
    s_r, s_l, s_k, s_x, t_r, t_l, k_l, x_l, rt, lt,
    tc, lc, rc, ltc, rtc, m_u,
    up, rs_u, u_row, u_cand, xy_row, xy,
    dp, rs_d, d_row, d_cand, dd_row, dd,
    rs_e, e_row, e_cand, e_all, z, zc, base, gb, x_near, p_one, ss, rs,
):
    n = lax.axis_index("node")
    s = lax.axis_index("slab")
    b = env_ref.shape[0]
    w = b // ns
    rows = pl.ds(pl.multiple_of(s * w, w), w)
    leaf = n >= 8

    loads = [
        pltpu.make_async_copy(t_hbm, t_ref, in_sem.at[0]),
        pltpu.make_async_copy(ops_hbm, ops_ref, in_sem.at[1]),
        pltpu.make_async_copy(env_hbm, env_ref, in_sem.at[2]),
        pltpu.make_async_copy(assign_hbm, assign_ref, in_sem.at[3]),
        pltpu.make_async_copy(parent_hbm, parent_ref, in_sem.at[4]),
    ]
    for load in (loads[0], loads[3], loads[4]):
        load.start()

    def block(j):
        return pl.ds(pl.multiple_of(j * w, w), w)

    c0 = jnp.where(n >= 4, 8, jnp.where(n >= 2, 4, jnp.where(n >= 1, 2, 1)))
    c1 = jnp.where(n >= 8, 8, jnp.where(n >= 1, 2 * c0, 2))
    p0 = jnp.where(n >= 8, 4, jnp.where(n >= 4, 2, jnp.where(n >= 2, 1, 0)))
    p1 = jnp.where(n >= 2, 2 * p0, jnp.where(n >= 1, 1, 0))

    barrier = pltpu.get_barrier_semaphore()

    def greet_slab(k, c):
        pl.semaphore_signal(barrier, inc=1, device_id=(n, lax.rem(s + k, ns)), device_id_type=MESH)
        return c

    def greet_node(m, c):
        pl.semaphore_signal(barrier, inc=1, device_id=(m, s), device_id_type=MESH)
        return c

    lax.fori_loop(1, ns, greet_slab, 0)
    lax.fori_loop(p0, p1, greet_node, 0)

    @pl.when(n >= 2)
    def _():
        def greet_child(m, c):
            to = jnp.where(m >= 12, s + 2 - 4 * lax.rem(s // 2, 2), s)
            pl.semaphore_signal(barrier, inc=1, device_id=(m, to), device_id_type=MESH)
            return c

        lax.fori_loop(c0, c1, greet_child, 0)

    @pl.when(n < 2)
    def _():
        def greet_all(k, c):
            m = c0 + k // ns
            pl.semaphore_signal(barrier, inc=1, device_id=(m, lax.rem(k, ns)), device_id_type=MESH)
            return c

        lax.fori_loop(0, (c1 - c0) * ns, greet_all, 0)

    @pl.when((n == 2) | (n == 3))
    def _():
        greet_node(5 - n, 0)

    pair_of_two = jnp.where((n == 2) | (n == 3), 1, 0)
    greetings = (ns - 1) + jnp.where((n >= 1) & (n < 4), ns, p1 - p0) + (c1 - c0) + pair_of_two

    def owned(m, j):
        return jnp.where(m >= 12, j + 2 - 4 * lax.rem(j // 2, 2), j)

    def peer(k):
        return lax.rem(s + 1 + lax.rem(k + ns // 2 - 2, ns - 1), ns)

    def remote(q, src, dst, to, slab, arrival=None):
        return pltpu.make_async_remote_copy(
            src_ref=src, dst_ref=dst, send_sem=ss.at[q], recv_sem=rs.at[q if arrival is None else arrival],
            device_id=(to, slab), device_id_type=MESH,
        )

    def arrived(q, like):
        remote(q, like, like, n, lax.rem(s + 1, ns)).wait_recv()

    def drained(q, like):
        remote(q, like, like, n, lax.rem(s + 1, ns)).wait_send()

    def slab_start(q, src_of, dst):
        def go(k, c):
            j = peer(k)
            remote(q, src_of(j), dst, n, j).start()
            return c

        lax.fori_loop(1, ns, go, 0)

    def node_start(q, src, dst, lo, hi, slab=s):
        def go(m, c):
            remote(q, src, dst, m, slab).start()
            return c

        lax.fori_loop(lo, hi, go, 0)

    others = pl.ds(0, ns - 1)
    other_rows = pl.ds(0, b - w)

    def spread(dst, i, x):
        dst.reshape(b * w, b)[pl.ds(i, b, stride=w), :] = x

    def a2a_start(q, src, dst):
        slab_start(q, lambda j: src.at[block(j)], dst.at[:, rows, :])
        dst[:, rows, :] = src[rows]

    def a2a_wait(q, dst):
        arrived(q, dst.at[:, other_rows, :])

    def a2a_drain(q, src):
        drained(q, src.at[other_rows])

    def part(i):
        return slice(i * b, (i + 1) * b)

    def sandwich(cat, turned, x, add=None):
        side = beside(x)
        weights = jnp.concatenate([side, side], axis=0)
        total = jnp.zeros((2 * b, 2 * b), F32)
        for i in range(0, w, 2):
            moved = []
            for k in (i, i + 1):
                both = dot(cat[part(k), :], weights)
                both = both[:, :b] + both[:, b:]
                if add is not None:
                    add[k] = add[k] + both
                moved.append(above(both))
            total = total + dot(jnp.concatenate(moved, axis=1), turned[i * b : (i + 2) * b, :])
        return quarters(total)

    def exact_sandwich(m, x):
        total = jnp.zeros((b, b), F32)
        for i in range(w):
            total = total + exact(exact(m[i], x), m[i], nt=True)
        return total

    def family(m):
        first = jnp.int32(NODES - 1)
        last = jnp.int32(0)
        for k in range(NODES - 1, 0, -1):
            first = jnp.where(parent_ref[k] == m, k, first)
        for k in range(1, NODES):
            last = jnp.where(parent_ref[k] == m, k, last)
        return first, last

    loads[0].wait()
    loads[1].start()
    loads[2].start()

    @pl.when(n < 8)
    def _():
        for i in range(w):
            spread(s_r, i, t_ref[part(i), :].T)

    for i in range(w):
        spread(s_l, i, t_ref[part(i), :])
    pl.semaphore_wait(barrier, greetings)

    @pl.when(n < 8)
    def _():
        a2a_start(A2A_R, s_r, t_r)

    a2a_start(A2A_L, s_l, t_l)
    for load in loads[1:]:
        load.wait()
    left_child, right_child = family(n)
    mine = parent_ref[n]
    eldest, _ = family(mine)
    side_of = jnp.where(eldest == n, 0, 1)
    first_id = assign_ref[0, n]
    second_id = assign_ref[1, n]
    op_p = ops_ref[first_id]
    op_q = ops_ref[second_id]
    for i in range(w):
        t = t_ref[part(i), :]
        tq = exact(t, op_q)
        v = jnp.where(leaf, t + tq, tq)
        spread(s_k, i, exact(op_p, v) + jnp.where(leaf, tq, 0.0))
    a2a_start(A2A_K, s_k, k_l)

    def right_forms():
        a2a_wait(A2A_R, t_r)
        for i in range(w):
            x = t_r[i].T
            rt[i] = x
            rtc[part(i), :] = beside(x)
        for i in range(w):
            rc[part(i), :] = beside(t_r[i])

    def left_forms():
        a2a_wait(A2A_L, t_l)
        for i in range(w):
            x = t_l[i].T
            lt[i] = x
            ltc[part(i), :] = beside(x)
        for i in range(w):
            lc[part(i), :] = beside(t_l[i])

    def own_forms():
        for i in range(w):
            tc[part(i), :] = beside(t_ref[part(i), :])

    def pair_square():
        a2a_wait(A2A_K, k_l)
        total = jnp.zeros((b, b), F32)
        for i in range(w):
            total = total + exact(k_l[i], t_l[i], nt=True)
        up[...] = total

    def pick_d(count):
        arrived(NODE_D, d_cand.at[pl.ds(0, count)])
        dd_row[...] = d_cand[mine, side_of]
        slab_start(AG_D, lambda j: dd_row, dd.at[rows, :])
        dd[rows, :] = dd_row[...]

    def gather_d():
        arrived(AG_D, dd.at[other_rows, :])

    def push_d():
        slab_start(RS_D, lambda j: dp.at[:, block(j), :], rs_d.at[s])
        rs_d[s] = dp[:, rows, :]

    def square_d():
        d = dd[...]
        dp[0] = sandwich(rtc, rc, d)
        dp[1] = sandwich(ltc, lc, d)
        push_d()

    def send_d():
        arrived(RS_D, rs_d.at[others])
        total = rs_d[0]
        for k in range(1, ns):
            total = total + rs_d[k]
        d_row[...] = total
        node_start(NODE_D, d_row, d_cand.at[n], c0, c1)

    def push_u():
        slab_start(RS_U, lambda j: up.at[block(owned(n, j)), :], rs_u.at[s])
        rs_u[s] = up[block(owned(n, s)), :]

    def send_u():
        arrived(RS_U, rs_u.at[others])
        total = rs_u[0]
        for k in range(1, ns):
            total = total + rs_u[k]
        u_row[...] = total
        node_start(NODE_U, u_row, u_cand.at[n], p0, p1, owned(n, s))

    def spread_u():
        slab_start(AG_U, lambda j: xy_row, xy.at[:, rows, :])
        xy[:, rows, :] = xy_row[...]

    def pick_u(count):
        arrived(NODE_U, u_cand.at[pl.ds(0, count)])
        xy_row[0] = u_cand[left_child]
        xy_row[1] = u_cand[right_child]
        spread_u()

    def push_merged():
        slot = jnp.where(n == 3, 1, 0)

        def go(k, c):
            j = lax.rem(s + k + ns // 2, ns)
            remote(MERGE, up.at[block(j), :], m_u.at[slot, s], n // 2, j, MERGE + slot).start()
            return c

        lax.fori_loop(0, ns, go, 0)

    def pick_merged(slot):
        arrived(MERGE + slot, m_u.at[slot])
        total = m_u[slot, 0]
        for k in range(1, ns):
            total = total + m_u[slot, k]
        xy_row[slot] = total

    def gather_u():
        arrived(AG_U, xy.at[:, other_rows, :])

    def square_u():
        up[...] = up[...] + (sandwich(rc, rtc, xy[0]) + sandwich(lc, ltc, xy[1], add=k_l))

    def move_left():
        x = above(xy[0])
        for i in range(w):
            spread(s_x, i, product(x, tc[part(i), :]))
        a2a_start(A2A_X, s_x, x_l)

    def push_energy(square):
        terms = dd[...] * square
        total = terms[0:w, :]
        for k in range(1, ns):
            total = total + terms[k * w : (k + 1) * w, :]
        rs_e[s] = total
        slab_start(SLAB_E, lambda j: rs_e.at[s], rs_e.at[s])

    def own_energy():
        arrived(SLAB_E, rs_e.at[others])
        total = rs_e[0]
        for k in range(1, ns):
            total = total + rs_e[k]
        return total

    def wait_total():
        arrived(NODE_F, e_all)

    def drain_first():
        a2a_drain(A2A_L, s_l)
        a2a_drain(A2A_K, s_k)

        @pl.when(n < 8)
        def _():
            a2a_drain(A2A_R, s_r)

    factor = b**0.75

    @pl.when(leaf)
    def _():
        a2a_wait(A2A_L, t_l)
        pair_square()
        push_u()
        send_u()
        drain_first()
        pick_d(4)
        gather_d()

    @pl.when((n >= 4) & (n < 8))
    def _():
        right_forms()
        left_forms()
        pair_square()
        own_forms()
        pick_u(8)
        gather_u()
        square_u()
        push_u()
        send_u()
        move_left()
        drain_first()
        pick_d(2)
        gather_d()
        square_d()
        send_d()
        wait_total()
        node_start(NODE_F, e_all, e_all, 2 * n, 2 * n + 2)

    @pl.when((n == 2) | (n == 3))
    def _():
        right_forms()
        left_forms()
        pair_square()
        own_forms()
        drain_first()
        pick_d(1)
        gather_d()
        square_d()
        pick_u(4)
        send_d()
        gather_u()
        square_u()
        push_merged()
        push_energy(up[...])
        move_left()
        e_row[...] = own_energy()
        e_cand[n] = e_row[...]
        node_start(NODE_E, e_row, e_cand.at[n], 5 - n, 6 - n)
        arrived(NODE_E, e_cand.at[pl.ds(0, 2)])
        e_all[...] = e_cand[1] + (e_cand[2] + e_cand[3])

        @pl.when(n == 2)
        def _():
            node_start(NODE_F, e_all, e_all, 4, 8)
            node_start(NODE_F, e_all, e_all, 1, 2)

    @pl.when(n == 1)
    def _():
        right_forms()
        left_forms()
        pick_d(1)
        gather_d()
        d = dd[...]
        dp[0] = exact_sandwich(rt, d)
        dp[1] = exact_sandwich(lt, d)
        push_d()
        send_d()
        pair_square()
        push_energy(up[...])
        own_forms()
        own = own_energy()
        arrived(NODE_E, e_cand.at[0])
        e_row[...] = own + e_cand[0]
        node_start(NODE_E, e_row, e_cand.at[n], 2, 4)
        drain_first()
        pick_merged(0)
        pick_merged(1)
        spread_u()
        gather_u()
        square_u()
        push_merged()
        move_left()
        wait_total()
        node_start(NODE_F, e_all, e_all, 0, 1)

    @pl.when(n == 0)
    def _():
        chips = ns // 2
        chip, core = s // 2, lax.rem(s, 2)
        near = [chip, lax.rem(chip + 2, chips), lax.rem(chip + chips - 2, chips)]
        z_peer = s + 2 - 4 * lax.rem(chip, 2)
        holders = [s, z_peer, lax.rem(s + chips, ns), lax.rem(z_peer + chips, ns)]
        kept = len(holders)

        dd[...] = env_ref[...]
        right_forms()
        dp[0] = exact_sandwich(rt, env_ref[...])
        dp[1] = jnp.zeros((b, b), F32)
        push_d()
        send_d()
        left_forms()
        d = above(env_ref[...] * factor)
        for i in range(w):
            x_l[i] = product(d, lc[part(i), :])
        slab_start(A2A_Z, lambda j: x_l.at[:, block(j), :], z.at[0, rows])
        z[0, rows] = x_l[:, rows, :]
        pair_square()
        push_energy(up[...] + sandwich(lc, ltc, op_q))
        e_row[...] = own_energy()
        node_start(NODE_E, e_row, e_cand.at[n], 1, 2)
        arrived(A2A_Z, z.at[0, other_rows])
        for k in range(1, kept):
            remote(COPIES, z.at[0], z.at[k], n, holders[k]).start()
        q_side = beside(op_q)
        q_weights = jnp.concatenate([q_side, q_side], axis=0)
        same = lax.broadcasted_iota(jnp.int32, (b, b), 0) == lax.broadcasted_iota(jnp.int32, (b, b), 1)
        p_one[...] = op_p + jnp.where(same, 1.0, 0.0)

        def chip_rows(m):
            return pl.ds(pl.multiple_of(m * (2 * w), 2 * w), 2 * w)

        p_near = above(jnp.concatenate([p_one[chip_rows(m), :] for m in near], axis=0))
        drain_first()
        drained(A2A_Z, x_l.at[:, other_rows, :])
        drained(RS_D, dp.at[:, other_rows, :])
        drained(NODE_D, d_row)
        drained(SLAB_E, rs_e.at[others])
        drained(NODE_E, e_row)
        arrived(COPIES, z.at[pl.ds(1, kept - 1)])
        drained(COPIES, z.at[pl.ds(1, kept - 1)])

        def known(q, c):
            side = beside(z.reshape(kept * b * w, b)[pl.ds((q // w) * (b * w) + lax.rem(q, w), b, stride=w), :])
            zc[q] = side
            moved = dot(side, q_weights)
            base[q] = product(p_near, beside(moved[:, :b] + moved[:, b:]))
            return c

        lax.fori_loop(0, kept * w, known, 0)

        pick_merged(0)
        mine_at = pl.ds(pl.multiple_of(core * w, w), w)
        ahead_at = pl.ds(pl.multiple_of((core + 4) * w, w), w)
        behind_at = pl.ds(pl.multiple_of((core + 2) * w, w), w)
        for c in range(2):
            remote(AG_U, xy_row.at[0], x_near.at[ahead_at, :], n, 2 * near[1] + c).start()
            remote(AG_U, xy_row.at[0], x_near.at[behind_at, :], n, 2 * near[2] + c).start()
        remote(AG_U, xy_row.at[0], x_near.at[mine_at, :], n, s + 1 - 2 * core).start()
        x_near[mine_at, :] = xy_row[0]
        arrived(AG_U, x_near.at[pl.ds(0, 5 * w), :])
        x = above(x_near[...])
        x_own = above(x_near[0 : 2 * w, :])

        def span(m):
            return pl.ds(pl.multiple_of(m * w, w), w)

        for k in range(kept):
            count = 6 if k < 2 else 2
            for i in range(w):
                q = k * w + i
                g = product(x if k < 2 else x_own, zc[q]) + base[q, 0 : count * w, :]
                for t in range(count):
                    gb[t, q] = g[t * w : (t + 1) * w, :]
            for t in range(2, count):
                remote(A2A_X, gb.at[t, pl.ds(k * w, w)], out_ref.at[span(holders[k])], n, 2 * near[t // 2] + t % 2).start()
        for k in range(kept):
            remote(A2A_X, gb.at[1 - core, pl.ds(k * w, w)], out_ref.at[span(holders[k])], n, s + 1 - 2 * core).start()
            out_ref[span(holders[k])] = gb[core, pl.ds(k * w, w)]
        wait_total()
        drained(AG_U, x_near.at[pl.ds(0, 5 * w), :])
        arrived(A2A_X, out_ref.at[pl.ds(0, 12 * w)])
        drained(A2A_X, out_ref.at[pl.ds(0, 12 * w)])

    @pl.when(n >= 1)
    def _():
        @pl.when(n < 8)
        def _():
            a2a_wait(A2A_X, x_l)

        d = above(dd[...] * factor)
        for i in range(w):
            side = beside(k_l[i] + jnp.where(n < 8, x_l[i], 0.0))
            out_ref.reshape(b * w, b)[pl.ds(i, b, stride=w), :] = product(d, side)

    @pl.when(leaf)
    def _():
        wait_total()

    en_ref[...] = jnp.sum(e_all[...], axis=(0, 1), keepdims=True)

    @pl.when((n >= 1) & (n < 8))
    def _():
        a2a_drain(A2A_X, s_x)
        drained(RS_D, dp.at[:, other_rows, :])
        drained(AG_U, xy.at[:, other_rows, :])

    @pl.when(n >= 1)
    def _():
        drained(AG_D, dd.at[other_rows, :])

    @pl.when(n >= 4)
    def _():
        drained(RS_U, up.at[other_rows, :])

    @pl.when((n >= 1) & (n < 4))
    def _():
        drained(MERGE, up)
        drained(SLAB_E, rs_e.at[others])

    @pl.when(n == 1)
    def _():
        drained(NODE_D, d_cand.at[pl.ds(0, 2)])
        drained(NODE_E, e_cand.at[pl.ds(0, 2)])
        drained(NODE_F, e_all)

    @pl.when((n == 2) | (n == 3))
    def _():
        drained(NODE_D, d_cand.at[pl.ds(0, 4)])
        drained(NODE_E, e_row)

    @pl.when(n == 2)
    def _():
        drained(NODE_F, e_cand.at[pl.ds(0, 5)])

    @pl.when((n >= 4) & (n < 8))
    def _():
        drained(NODE_D, d_cand.at[pl.ds(0, 8)])
        drained(NODE_U, u_cand.at[pl.ds(0, 2)])
        drained(NODE_F, e_cand.at[pl.ds(0, 2)])

    @pl.when(leaf)
    def _():
        drained(NODE_U, u_cand.at[pl.ds(0, 4)])


def per_device(ns, tensors, ops, assign, parent, env):
    b = env.shape[0]
    w = b // ns
    stack = pltpu.VMEM((w * b, b), F32)
    full = pltpu.VMEM((b, w, b), F32)
    form = pltpu.VMEM((w, b, b), F32)
    cat = pltpu.VMEM((w * b, 2 * b), BF16)
    square = pltpu.VMEM((b, b), F32)
    slab = pltpu.VMEM((w, b), F32)
    two = pltpu.VMEM((2, w, b), F32)
    hbm = pl.BlockSpec(memory_space=pl.ANY)
    vmem = pl.BlockSpec(memory_space=pltpu.VMEM)
    grad, energy = pl.pallas_call(
        functools.partial(kernel, ns),
        out_shape=(pltpu.VMEM((b, w, b), F32), pltpu.VMEM((1, 1), F32)),
        in_specs=[hbm] * 5,
        out_specs=(vmem, vmem),
        scratch_shapes=[
            stack, pltpu.VMEM(ops.shape, F32), square,
            pltpu.SMEM((2, NODES), jnp.int32), pltpu.SMEM((NODES,), jnp.int32), pltpu.SemaphoreType.DMA((5,)),
            full, full, full, full, form, form, form, form, form, form,
            cat, cat, cat, cat, cat, pltpu.VMEM((2, ns, w, b), F32),
            square, pltpu.VMEM((ns, w, b), F32), slab, pltpu.VMEM((NODES, w, b), F32), two, pltpu.VMEM((2, b, b), F32),
            pltpu.VMEM((2, b, b), F32), pltpu.VMEM((ns, 2, w, b), F32), two,
            pltpu.VMEM((NODES, 2, w, b), F32), slab, square,
            pltpu.VMEM((ns, w, b), F32), slab, pltpu.VMEM((NODES, w, b), F32), slab,
            pltpu.VMEM((4, b, w, b), F32), pltpu.VMEM((4 * w, b, 2 * b), BF16), pltpu.VMEM((4 * w, 6 * w, b), F32),
            pltpu.VMEM((6, 4 * w, w, b), F32), pltpu.VMEM((6 * w, b), F32), square,
            pltpu.SemaphoreType.DMA((COUNT,)), pltpu.SemaphoreType.DMA((COUNT,)),
        ],
        compiler_params=pltpu.CompilerParams(collective_id=0, has_side_effects=True),
    )(tensors.reshape(w * b, b), ops, env, assign.T, parent)
    return grad[None], energy[0, 0]


def solution(mesh):
    return jax.shard_map(
        functools.partial(per_device, mesh.shape["slab"]),
        mesh=mesh,
        in_specs=(P("node", "slab", None, None), P(), P(), P(), P()),
        out_specs=(P("node", None, "slab", None), P()),
        check_vma=False,
    )
```

```python
import functools

import jax
import jax.numpy as jnp
from jax import lax
from jax.experimental import pallas as pl
from jax.experimental.pallas import tpu as pltpu
from jax.sharding import PartitionSpec as P

NODES = 16
MESH = pl.DeviceIdType.MESH
F32 = jnp.float32
BF16 = jnp.bfloat16

A2A_R, A2A_L, A2A_K, A2A_X, RS_U, RS_D, AG_U, AG_D, SLAB_E, NODE_U, NODE_D, NODE_E, NODE_F, A2A_Z, MERGE, MERGE2, COPIES, COUNT = range(18)


def split(x):
    hi = x.astype(BF16)
    return hi, (x - hi.astype(F32)).astype(BF16)


def beside(x):
    return jnp.concatenate(split(x), axis=1)


def above(x):
    return jnp.concatenate(split(x), axis=0)


def dot(a, b, nt=False, precision=None):
    dims = (((1,), (1 if nt else 0,)), ((), ()))
    return lax.dot_general(a, b, dims, preferred_element_type=F32, precision=precision)


def exact(a, b, nt=False):
    return dot(a, b, nt, lax.Precision.HIGHEST)


def quarters(x):
    h, w = x.shape[0] // 2, x.shape[1] // 2
    return (x[:h, :w] + x[:h, w:]) + (x[h:, :w] + x[h:, w:])


def product(x, y):
    return quarters(dot(x, y))


def kernel(
    ns, t_hbm, ops_hbm, env_hbm, assign_hbm, parent_hbm, out_ref, en_ref,
    t_ref, ops_ref, env_ref, assign_ref, parent_ref, in_sem,
    s_r, s_l, s_k, s_x, t_r, t_l, k_l, x_l, rt, lt,
    tc, lc, rc, ltc, rtc, m_u,
    up, rs_u, u_row, u_cand, xy_row, xy,
    dp, rs_d, d_row, d_cand, dd_row, dd,
    rs_e, e_row, e_cand, e_all, z, zc, base, gb, x_near, p_one, ss, rs,
):
    n = lax.axis_index("node")
    s = lax.axis_index("slab")
    b = env_ref.shape[0]
    w = b // ns
    rows = pl.ds(pl.multiple_of(s * w, w), w)
    leaf = n >= 8

    loads = [
        pltpu.make_async_copy(t_hbm, t_ref, in_sem.at[0]),
        pltpu.make_async_copy(ops_hbm, ops_ref, in_sem.at[1]),
        pltpu.make_async_copy(env_hbm, env_ref, in_sem.at[2]),
        pltpu.make_async_copy(assign_hbm, assign_ref, in_sem.at[3]),
        pltpu.make_async_copy(parent_hbm, parent_ref, in_sem.at[4]),
    ]
    for load in (loads[0], loads[3], loads[4]):
        load.start()

    def block(j):
        return pl.ds(pl.multiple_of(j * w, w), w)

    c0 = jnp.where(n >= 4, 8, jnp.where(n >= 2, 4, jnp.where(n >= 1, 2, 1)))
    c1 = jnp.where(n >= 8, 8, jnp.where(n >= 1, 2 * c0, 2))
    p0 = jnp.where(n >= 8, 4, jnp.where(n >= 4, 2, jnp.where(n >= 2, 1, 0)))
    p1 = jnp.where(n >= 2, 2 * p0, jnp.where(n >= 1, 1, 0))

    barrier = pltpu.get_barrier_semaphore()

    def greet_slab(k, c):
        pl.semaphore_signal(barrier, inc=1, device_id=(n, lax.rem(s + k, ns)), device_id_type=MESH)
        return c

    def greet_node(m, c):
        pl.semaphore_signal(barrier, inc=1, device_id=(m, s), device_id_type=MESH)
        return c

    lax.fori_loop(1, ns, greet_slab, 0)
    lax.fori_loop(p0, p1, greet_node, 0)

    @pl.when(n >= 2)
    def _():
        def greet_child(m, c):
            to = jnp.where(m >= 12, s + 2 - 4 * lax.rem(s // 2, 2), s)
            pl.semaphore_signal(barrier, inc=1, device_id=(m, to), device_id_type=MESH)
            return c

        lax.fori_loop(c0, c1, greet_child, 0)

    @pl.when(n < 2)
    def _():
        def greet_all(k, c):
            m = c0 + k // ns
            pl.semaphore_signal(barrier, inc=1, device_id=(m, lax.rem(k, ns)), device_id_type=MESH)
            return c

        lax.fori_loop(0, (c1 - c0) * ns, greet_all, 0)

    @pl.when((n == 2) | (n == 3))
    def _():
        greet_node(5 - n, 0)

    pair_of_two = jnp.where((n == 2) | (n == 3), 1, 0)
    greetings = (ns - 1) + jnp.where((n >= 1) & (n < 4), ns, p1 - p0) + (c1 - c0) + pair_of_two

    def owned(m, j):
        return jnp.where(m >= 12, j + 2 - 4 * lax.rem(j // 2, 2), j)

    def peer(k):
        return lax.rem(s + 1 + lax.rem(k + ns // 2 - 2, ns - 1), ns)

    def remote(q, src, dst, to, slab, arrival=None):
        return pltpu.make_async_remote_copy(
            src_ref=src, dst_ref=dst, send_sem=ss.at[q], recv_sem=rs.at[q if arrival is None else arrival],
            device_id=(to, slab), device_id_type=MESH,
        )

    def arrived(q, like):
        remote(q, like, like, n, lax.rem(s + 1, ns)).wait_recv()

    def drained(q, like):
        remote(q, like, like, n, lax.rem(s + 1, ns)).wait_send()

    def slab_start(q, src_of, dst):
        def go(k, c):
            j = peer(k)
            remote(q, src_of(j), dst, n, j).start()
            return c

        lax.fori_loop(1, ns, go, 0)

    def node_start(q, src, dst, lo, hi, slab=s):
        def go(m, c):
            remote(q, src, dst, m, slab).start()
            return c

        lax.fori_loop(lo, hi, go, 0)

    others = pl.ds(0, ns - 1)
    other_rows = pl.ds(0, b - w)

    def spread(dst, i, x):
        dst.reshape(b * w, b)[pl.ds(i, b, stride=w), :] = x

    def a2a_start(q, src, dst):
        slab_start(q, lambda j: src.at[block(j)], dst.at[:, rows, :])
        dst[:, rows, :] = src[rows]

    def a2a_wait(q, dst):
        arrived(q, dst.at[:, other_rows, :])

    def a2a_drain(q, src):
        drained(q, src.at[other_rows])

    def part(i):
        return slice(i * b, (i + 1) * b)

    def sandwich(cat, turned, x, add=None):
        side = beside(x)
        weights = jnp.concatenate([side, side], axis=0)
        total = jnp.zeros((2 * b, 2 * b), F32)
        for i in range(0, w, 2):
            moved = []
            for k in (i, i + 1):
                both = dot(cat[part(k), :], weights)
                both = both[:, :b] + both[:, b:]
                if add is not None:
                    add[k] = add[k] + both
                moved.append(above(both))
            total = total + dot(jnp.concatenate(moved, axis=1), turned[i * b : (i + 2) * b, :])
        return quarters(total)

    def exact_sandwich(m, x):
        total = jnp.zeros((b, b), F32)
        for i in range(w):
            total = total + exact(exact(m[i], x), m[i], nt=True)
        return total

    def family(m):
        first = jnp.int32(NODES - 1)
        last = jnp.int32(0)
        for k in range(NODES - 1, 0, -1):
            first = jnp.where(parent_ref[k] == m, k, first)
        for k in range(1, NODES):
            last = jnp.where(parent_ref[k] == m, k, last)
        return first, last

    loads[0].wait()
    loads[1].start()
    loads[2].start()

    @pl.when(n < 8)
    def _():
        for i in range(w):
            spread(s_r, i, t_ref[part(i), :].T)

    for i in range(w):
        spread(s_l, i, t_ref[part(i), :])
    pl.semaphore_wait(barrier, greetings)

    @pl.when(n < 8)
    def _():
        a2a_start(A2A_R, s_r, t_r)

    a2a_start(A2A_L, s_l, t_l)
    for load in loads[1:]:
        load.wait()
    left_child, right_child = family(n)
    mine = parent_ref[n]
    eldest, _ = family(mine)
    side_of = jnp.where(eldest == n, 0, 1)
    first_id = assign_ref[0, n]
    second_id = assign_ref[1, n]
    op_p = ops_ref[first_id]
    op_q = ops_ref[second_id]
    for i in range(w):
        t = t_ref[part(i), :]
        tq = exact(t, op_q)
        v = jnp.where(leaf, t + tq, tq)
        spread(s_k, i, exact(op_p, v) + jnp.where(leaf, tq, 0.0))
    a2a_start(A2A_K, s_k, k_l)

    def right_forms():
        a2a_wait(A2A_R, t_r)
        for i in range(w):
            x = t_r[i].T
            rt[i] = x
            rtc[part(i), :] = beside(x)
        for i in range(w):
            rc[part(i), :] = beside(t_r[i])

    def left_forms():
        a2a_wait(A2A_L, t_l)
        for i in range(w):
            x = t_l[i].T
            lt[i] = x
            ltc[part(i), :] = beside(x)
        for i in range(w):
            lc[part(i), :] = beside(t_l[i])

    def own_forms():
        for i in range(w):
            tc[part(i), :] = beside(t_ref[part(i), :])

    def pair_square():
        a2a_wait(A2A_K, k_l)
        total = jnp.zeros((b, b), F32)
        for i in range(w):
            total = total + exact(k_l[i], t_l[i], nt=True)
        up[...] = total

    def pick_d(count):
        arrived(NODE_D, d_cand.at[pl.ds(0, count)])
        dd_row[...] = d_cand[mine, side_of]
        slab_start(AG_D, lambda j: dd_row, dd.at[rows, :])
        dd[rows, :] = dd_row[...]

    def gather_d():
        arrived(AG_D, dd.at[other_rows, :])

    def push_d():
        slab_start(RS_D, lambda j: dp.at[:, block(j), :], rs_d.at[s])
        rs_d[s] = dp[:, rows, :]

    def square_d():
        d = dd[...]
        dp[0] = sandwich(rtc, rc, d)
        dp[1] = sandwich(ltc, lc, d)
        push_d()

    def send_d():
        arrived(RS_D, rs_d.at[others])
        total = rs_d[0]
        for k in range(1, ns):
            total = total + rs_d[k]
        d_row[...] = total
        node_start(NODE_D, d_row, d_cand.at[n], c0, c1)

    def push_u():
        slab_start(RS_U, lambda j: up.at[block(owned(n, j)), :], rs_u.at[s])
        rs_u[s] = up[block(owned(n, s)), :]

    def send_u():
        arrived(RS_U, rs_u.at[others])
        total = rs_u[0]
        for k in range(1, ns):
            total = total + rs_u[k]
        u_row[...] = total
        node_start(NODE_U, u_row, u_cand.at[n], p0, p1, owned(n, s))

    def spread_u():
        slab_start(AG_U, lambda j: xy_row, xy.at[:, rows, :])
        xy[:, rows, :] = xy_row[...]

    def pick_u(count):
        arrived(NODE_U, u_cand.at[pl.ds(0, count)])
        xy_row[0] = u_cand[left_child]
        xy_row[1] = u_cand[right_child]
        spread_u()

    def push_merged():
        slot = jnp.where(n == 3, 1, 0)

        def go(k, c):
            j = lax.rem(s + k + ns // 2, ns)
            remote(MERGE, up.at[block(j), :], m_u.at[slot, s], n // 2, j, MERGE + slot).start()
            return c

        lax.fori_loop(0, ns, go, 0)

    def pick_merged(slot):
        arrived(MERGE + slot, m_u.at[slot])
        total = m_u[slot, 0]
        for k in range(1, ns):
            total = total + m_u[slot, k]
        xy_row[slot] = total

    def gather_u():
        arrived(AG_U, xy.at[:, other_rows, :])

    def square_u():
        up[...] = up[...] + (sandwich(rc, rtc, xy[0]) + sandwich(lc, ltc, xy[1], add=k_l))

    def move_left():
        x = above(xy[0])
        for i in range(w):
            spread(s_x, i, product(x, tc[part(i), :]))
        a2a_start(A2A_X, s_x, x_l)

    def push_energy(square):
        terms = dd[...] * square
        total = terms[0:w, :]
        for k in range(1, ns):
            total = total + terms[k * w : (k + 1) * w, :]
        rs_e[s] = total
        slab_start(SLAB_E, lambda j: rs_e.at[s], rs_e.at[s])

    def own_energy():
        arrived(SLAB_E, rs_e.at[others])
        total = rs_e[0]
        for k in range(1, ns):
            total = total + rs_e[k]
        return total

    def wait_total():
        arrived(NODE_F, e_all)

    def drain_first():
        a2a_drain(A2A_L, s_l)
        a2a_drain(A2A_K, s_k)

        @pl.when(n < 8)
        def _():
            a2a_drain(A2A_R, s_r)

    factor = b**0.75

    @pl.when(leaf)
    def _():
        a2a_wait(A2A_L, t_l)
        pair_square()
        push_u()
        send_u()
        drain_first()
        pick_d(4)
        gather_d()

    @pl.when((n >= 4) & (n < 8))
    def _():
        right_forms()
        left_forms()
        pair_square()
        own_forms()
        pick_u(8)
        gather_u()
        square_u()
        push_u()
        send_u()
        move_left()
        drain_first()
        pick_d(2)
        gather_d()
        square_d()
        send_d()
        wait_total()
        node_start(NODE_F, e_all, e_all, 2 * n, 2 * n + 2)

    @pl.when((n == 2) | (n == 3))
    def _():
        right_forms()
        left_forms()
        pair_square()
        own_forms()
        drain_first()
        pick_d(1)
        gather_d()
        pick_u(4)
        square_d()
        gather_u()
        square_u()
        push_merged()
        send_d()
        push_energy(up[...])
        move_left()
        e_row[...] = own_energy()
        e_cand[n] = e_row[...]
        node_start(NODE_E, e_row, e_cand.at[n], 5 - n, 6 - n)
        arrived(NODE_E, e_cand.at[pl.ds(0, 2)])
        e_all[...] = e_cand[1] + (e_cand[2] + e_cand[3])

        @pl.when(n == 2)
        def _():
            node_start(NODE_F, e_all, e_all, 4, 8)
            node_start(NODE_F, e_all, e_all, 1, 2)

    @pl.when(n == 1)
    def _():
        right_forms()
        left_forms()
        pick_d(1)
        gather_d()
        d = dd[...]
        dp[0] = exact_sandwich(rt, d)
        dp[1] = exact_sandwich(lt, d)
        push_d()
        send_d()
        pair_square()
        push_energy(up[...])
        own_forms()
        own = own_energy()
        arrived(NODE_E, e_cand.at[0])
        e_row[...] = own + e_cand[0]
        node_start(NODE_E, e_row, e_cand.at[n], 2, 4)
        drain_first()
        pick_merged(0)
        pick_merged(1)
        spread_u()
        gather_u()
        square_u()
        push_merged()
        move_left()
        wait_total()
        node_start(NODE_F, e_all, e_all, 0, 1)

    @pl.when(n == 0)
    def _():
        chips = ns // 2
        chip, core = s // 2, lax.rem(s, 2)
        near = [chip, lax.rem(chip + 2, chips), lax.rem(chip + chips - 2, chips)]
        z_peer = s + 2 - 4 * lax.rem(chip, 2)
        holders = [s, z_peer, lax.rem(s + chips, ns), lax.rem(z_peer + chips, ns)]
        kept = len(holders)

        dd[...] = env_ref[...]
        right_forms()
        dp[0] = exact_sandwich(rt, env_ref[...])
        dp[1] = jnp.zeros((b, b), F32)
        push_d()
        send_d()
        left_forms()
        d = above(env_ref[...] * factor)
        for i in range(w):
            x_l[i] = product(d, lc[part(i), :])
        slab_start(A2A_Z, lambda j: x_l.at[:, block(j), :], z.at[0, rows])
        z[0, rows] = x_l[:, rows, :]
        pair_square()
        push_energy(up[...] + sandwich(lc, ltc, op_q))
        e_row[...] = own_energy()
        node_start(NODE_E, e_row, e_cand.at[n], 1, 2)
        arrived(A2A_Z, z.at[0, other_rows])
        for k in range(1, kept):
            remote(COPIES, z.at[0], z.at[k], n, holders[k]).start()
        q_side = beside(op_q)
        q_weights = jnp.concatenate([q_side, q_side], axis=0)
        same = lax.broadcasted_iota(jnp.int32, (b, b), 0) == lax.broadcasted_iota(jnp.int32, (b, b), 1)
        p_one[...] = op_p + jnp.where(same, 1.0, 0.0)

        def chip_rows(m):
            return pl.ds(pl.multiple_of(m * (2 * w), 2 * w), 2 * w)

        p_near = above(jnp.concatenate([p_one[chip_rows(m), :] for m in near], axis=0))
        drain_first()
        drained(A2A_Z, x_l.at[:, other_rows, :])
        drained(RS_D, dp.at[:, other_rows, :])
        drained(NODE_D, d_row)
        drained(SLAB_E, rs_e.at[others])
        drained(NODE_E, e_row)

        def known(q, c):
            side = beside(z.reshape(kept * b * w, b)[pl.ds((q // w) * (b * w) + lax.rem(q, w), b, stride=w), :])
            zc[q] = side
            moved = dot(side, q_weights)
            base[q] = product(p_near, beside(moved[:, :b] + moved[:, b:]))
            return c

        lax.fori_loop(0, w, known, 0)
        arrived(COPIES, z.at[pl.ds(1, kept - 1)])
        drained(COPIES, z.at[pl.ds(1, kept - 1)])
        lax.fori_loop(w, kept * w, known, 0)

        pick_merged(0)
        mine_at = pl.ds(pl.multiple_of(core * w, w), w)
        ahead_at = pl.ds(pl.multiple_of((core + 4) * w, w), w)
        behind_at = pl.ds(pl.multiple_of((core + 2) * w, w), w)
        for c in range(2):
            remote(AG_U, xy_row.at[0], x_near.at[ahead_at, :], n, 2 * near[1] + c).start()
            remote(AG_U, xy_row.at[0], x_near.at[behind_at, :], n, 2 * near[2] + c).start()
        remote(AG_U, xy_row.at[0], x_near.at[mine_at, :], n, s + 1 - 2 * core).start()
        x_near[mine_at, :] = xy_row[0]
        arrived(AG_U, x_near.at[pl.ds(0, 5 * w), :])
        x = above(x_near[...])
        x_own = above(x_near[0 : 2 * w, :])

        def span(m):
            return pl.ds(pl.multiple_of(m * w, w), w)

        for k in range(kept):
            count = 6 if k < 2 else 2
            for i in range(w):
                q = k * w + i
                g = product(x if k < 2 else x_own, zc[q]) + base[q, 0 : count * w, :]
                for t in range(count):
                    gb[t, q] = g[t * w : (t + 1) * w, :]
            for t in range(2, count):
                remote(A2A_X, gb.at[t, pl.ds(k * w, w)], out_ref.at[span(holders[k])], n, 2 * near[t // 2] + t % 2).start()
        for k in range(kept):
            remote(A2A_X, gb.at[1 - core, pl.ds(k * w, w)], out_ref.at[span(holders[k])], n, s + 1 - 2 * core).start()
            out_ref[span(holders[k])] = gb[core, pl.ds(k * w, w)]
        wait_total()
        drained(AG_U, x_near.at[pl.ds(0, 5 * w), :])
        arrived(A2A_X, out_ref.at[pl.ds(0, 12 * w)])
        drained(A2A_X, out_ref.at[pl.ds(0, 12 * w)])

    @pl.when(n >= 1)
    def _():
        @pl.when(n < 8)
        def _():
            a2a_wait(A2A_X, x_l)

        d = above(dd[...] * factor)
        for i in range(w):
            side = beside(k_l[i] + jnp.where(n < 8, x_l[i], 0.0))
            out_ref.reshape(b * w, b)[pl.ds(i, b, stride=w), :] = product(d, side)

    @pl.when(leaf)
    def _():
        wait_total()

    en_ref[...] = jnp.sum(e_all[...], axis=(0, 1), keepdims=True)

    @pl.when((n >= 1) & (n < 8))
    def _():
        a2a_drain(A2A_X, s_x)
        drained(RS_D, dp.at[:, other_rows, :])
        drained(AG_U, xy.at[:, other_rows, :])

    @pl.when(n >= 1)
    def _():
        drained(AG_D, dd.at[other_rows, :])

    @pl.when(n >= 4)
    def _():
        drained(RS_U, up.at[other_rows, :])

    @pl.when((n >= 1) & (n < 4))
    def _():
        drained(MERGE, up)
        drained(SLAB_E, rs_e.at[others])

    @pl.when(n == 1)
    def _():
        drained(NODE_D, d_cand.at[pl.ds(0, 2)])
        drained(NODE_E, e_cand.at[pl.ds(0, 2)])
        drained(NODE_F, e_all)

    @pl.when((n == 2) | (n == 3))
    def _():
        drained(NODE_D, d_cand.at[pl.ds(0, 4)])
        drained(NODE_E, e_row)

    @pl.when(n == 2)
    def _():
        drained(NODE_F, e_cand.at[pl.ds(0, 5)])

    @pl.when((n >= 4) & (n < 8))
    def _():
        drained(NODE_D, d_cand.at[pl.ds(0, 8)])
        drained(NODE_U, u_cand.at[pl.ds(0, 2)])
        drained(NODE_F, e_cand.at[pl.ds(0, 2)])

    @pl.when(leaf)
    def _():
        drained(NODE_U, u_cand.at[pl.ds(0, 4)])


def per_device(ns, tensors, ops, assign, parent, env):
    b = env.shape[0]
    w = b // ns
    stack = pltpu.VMEM((w * b, b), F32)
    full = pltpu.VMEM((b, w, b), F32)
    form = pltpu.VMEM((w, b, b), F32)
    cat = pltpu.VMEM((w * b, 2 * b), BF16)
    square = pltpu.VMEM((b, b), F32)
    slab = pltpu.VMEM((w, b), F32)
    two = pltpu.VMEM((2, w, b), F32)
    hbm = pl.BlockSpec(memory_space=pl.ANY)
    vmem = pl.BlockSpec(memory_space=pltpu.VMEM)
    grad, energy = pl.pallas_call(
        functools.partial(kernel, ns),
        out_shape=(pltpu.VMEM((b, w, b), F32), pltpu.VMEM((1, 1), F32)),
        in_specs=[hbm] * 5,
        out_specs=(vmem, vmem),
        scratch_shapes=[
            stack, pltpu.VMEM(ops.shape, F32), square,
            pltpu.SMEM((2, NODES), jnp.int32), pltpu.SMEM((NODES,), jnp.int32), pltpu.SemaphoreType.DMA((5,)),
            full, full, full, full, form, form, form, form, form, form,
            cat, cat, cat, cat, cat, pltpu.VMEM((2, ns, w, b), F32),
            square, pltpu.VMEM((ns, w, b), F32), slab, pltpu.VMEM((NODES, w, b), F32), two, pltpu.VMEM((2, b, b), F32),
            pltpu.VMEM((2, b, b), F32), pltpu.VMEM((ns, 2, w, b), F32), two,
            pltpu.VMEM((NODES, 2, w, b), F32), slab, square,
            pltpu.VMEM((ns, w, b), F32), slab, pltpu.VMEM((NODES, w, b), F32), slab,
            pltpu.VMEM((4, b, w, b), F32), pltpu.VMEM((4 * w, b, 2 * b), BF16), pltpu.VMEM((4 * w, 6 * w, b), F32),
            pltpu.VMEM((6, 4 * w, w, b), F32), pltpu.VMEM((6 * w, b), F32), square,
            pltpu.SemaphoreType.DMA((COUNT,)), pltpu.SemaphoreType.DMA((COUNT,)),
        ],
        compiler_params=pltpu.CompilerParams(collective_id=0, has_side_effects=True),
    )(tensors.reshape(w * b, b), ops, env, assign.T, parent)
    return grad[None], energy[0, 0]


def solution(mesh):
    return jax.shard_map(
        functools.partial(per_device, mesh.shape["slab"]),
        mesh=mesh,
        in_specs=(P("node", "slab", None, None), P(), P(), P(), P()),
        out_specs=(P("node", None, "slab", None), P()),
        check_vma=False,
    )
```

```python
import functools

import jax
import jax.numpy as jnp
from jax import lax
from jax.experimental import pallas as pl
from jax.experimental.pallas import tpu as pltpu
from jax.sharding import PartitionSpec as P

NODES = 16
MESH = pl.DeviceIdType.MESH
F32 = jnp.float32
BF16 = jnp.bfloat16

A2A_R, A2A_L, A2A_K, A2A_X, RS_U, RS_D, AG_U, AG_D, SLAB_E, NODE_U, NODE_D, NODE_E, NODE_F, A2A_Z, MERGE, MERGE2, COPIES, COUNT = range(18)


def split(x):
    hi = x.astype(BF16)
    return hi, (x - hi.astype(F32)).astype(BF16)


def beside(x):
    return jnp.concatenate(split(x), axis=1)


def above(x):
    return jnp.concatenate(split(x), axis=0)


def dot(a, b, nt=False, precision=None):
    dims = (((1,), (1 if nt else 0,)), ((), ()))
    return lax.dot_general(a, b, dims, preferred_element_type=F32, precision=precision)


def exact(a, b, nt=False):
    return dot(a, b, nt, lax.Precision.HIGHEST)


def quarters(x):
    h, w = x.shape[0] // 2, x.shape[1] // 2
    return (x[:h, :w] + x[:h, w:]) + (x[h:, :w] + x[h:, w:])


def product(x, y):
    return quarters(dot(x, y))


def kernel(
    ns, t_hbm, ops_hbm, env_hbm, assign_hbm, parent_hbm, out_ref, en_ref,
    t_ref, ops_ref, env_ref, assign_ref, parent_ref, in_sem,
    s_r, s_l, s_k, s_x, t_r, t_l, k_l, x_l, rt, lt,
    tc, lc, rc, ltc, rtc, m_u,
    up, rs_u, u_row, u_cand, xy_row, xy,
    dp, rs_d, d_row, d_cand, dd_row, dd,
    rs_e, e_row, e_cand, e_all, z, zc, base, gb, x_near, p_one, ss, rs,
):
    n = lax.axis_index("node")
    s = lax.axis_index("slab")
    b = env_ref.shape[0]
    w = b // ns
    rows = pl.ds(pl.multiple_of(s * w, w), w)
    leaf = n >= 8

    loads = [
        pltpu.make_async_copy(t_hbm, t_ref, in_sem.at[0]),
        pltpu.make_async_copy(ops_hbm, ops_ref, in_sem.at[1]),
        pltpu.make_async_copy(env_hbm, env_ref, in_sem.at[2]),
        pltpu.make_async_copy(assign_hbm, assign_ref, in_sem.at[3]),
        pltpu.make_async_copy(parent_hbm, parent_ref, in_sem.at[4]),
    ]
    for load in loads:
        load.start()

    def block(j):
        return pl.ds(pl.multiple_of(j * w, w), w)

    c0 = jnp.where(n >= 4, 8, jnp.where(n >= 2, 4, jnp.where(n >= 1, 2, 1)))
    c1 = jnp.where(n >= 8, 8, jnp.where(n >= 1, 2 * c0, 2))
    p0 = jnp.where(n >= 8, 4, jnp.where(n >= 4, 2, jnp.where(n >= 2, 1, 0)))
    p1 = jnp.where(n >= 2, 2 * p0, jnp.where(n >= 1, 1, 0))

    barrier = pltpu.get_barrier_semaphore()

    def greet_slab(k, c):
        pl.semaphore_signal(barrier, inc=1, device_id=(n, lax.rem(s + k, ns)), device_id_type=MESH)
        return c

    def greet_node(m, c):
        pl.semaphore_signal(barrier, inc=1, device_id=(m, s), device_id_type=MESH)
        return c

    lax.fori_loop(1, ns, greet_slab, 0)
    lax.fori_loop(p0, p1, greet_node, 0)

    @pl.when(n >= 2)
    def _():
        def greet_child(m, c):
            to = jnp.where(m >= 12, s + 2 - 4 * lax.rem(s // 2, 2), s)
            pl.semaphore_signal(barrier, inc=1, device_id=(m, to), device_id_type=MESH)
            return c

        lax.fori_loop(c0, c1, greet_child, 0)

    @pl.when(n < 2)
    def _():
        def greet_all(k, c):
            m = c0 + k // ns
            pl.semaphore_signal(barrier, inc=1, device_id=(m, lax.rem(k, ns)), device_id_type=MESH)
            return c

        lax.fori_loop(0, (c1 - c0) * ns, greet_all, 0)

    @pl.when((n == 2) | (n == 3))
    def _():
        greet_node(5 - n, 0)

    pair_of_two = jnp.where((n == 2) | (n == 3), 1, 0)
    greetings = (ns - 1) + jnp.where((n >= 1) & (n < 4), ns, p1 - p0) + (c1 - c0) + pair_of_two

    def owned(m, j):
        return jnp.where(m >= 12, j + 2 - 4 * lax.rem(j // 2, 2), j)

    def peer(k):
        return lax.rem(s + 1 + lax.rem(k + ns // 2 - 2, ns - 1), ns)

    def remote(q, src, dst, to, slab, arrival=None):
        return pltpu.make_async_remote_copy(
            src_ref=src, dst_ref=dst, send_sem=ss.at[q], recv_sem=rs.at[q if arrival is None else arrival],
            device_id=(to, slab), device_id_type=MESH,
        )

    def arrived(q, like):
        remote(q, like, like, n, lax.rem(s + 1, ns)).wait_recv()

    def drained(q, like):
        remote(q, like, like, n, lax.rem(s + 1, ns)).wait_send()

    def slab_start(q, src_of, dst):
        def go(k, c):
            j = peer(k)
            remote(q, src_of(j), dst, n, j).start()
            return c

        lax.fori_loop(1, ns, go, 0)

    def node_start(q, src, dst, lo, hi, slab=s):
        def go(m, c):
            remote(q, src, dst, m, slab).start()
            return c

        lax.fori_loop(lo, hi, go, 0)

    others = pl.ds(0, ns - 1)
    other_rows = pl.ds(0, b - w)

    def spread(dst, i, x):
        dst.reshape(b * w, b)[pl.ds(i, b, stride=w), :] = x

    def a2a_start(q, src, dst):
        slab_start(q, lambda j: src.at[block(j)], dst.at[:, rows, :])
        dst[:, rows, :] = src[rows]

    def a2a_wait(q, dst):
        arrived(q, dst.at[:, other_rows, :])

    def a2a_drain(q, src):
        drained(q, src.at[other_rows])

    def part(i):
        return slice(i * b, (i + 1) * b)

    def sandwich(cat, turned, x, add=None):
        side = beside(x)
        weights = jnp.concatenate([side, side], axis=0)
        total = jnp.zeros((2 * b, 2 * b), F32)
        for i in range(0, w, 2):
            moved = []
            for k in (i, i + 1):
                both = dot(cat[part(k), :], weights)
                both = both[:, :b] + both[:, b:]
                if add is not None:
                    add[k] = add[k] + both
                moved.append(above(both))
            total = total + dot(jnp.concatenate(moved, axis=1), turned[i * b : (i + 2) * b, :])
        return quarters(total)

    def exact_sandwich(m, x):
        total = jnp.zeros((b, b), F32)
        for i in range(w):
            total = total + exact(exact(m[i], x), m[i], nt=True)
        return total

    def family(m):
        first = jnp.int32(NODES - 1)
        last = jnp.int32(0)
        for k in range(NODES - 1, 0, -1):
            first = jnp.where(parent_ref[k] == m, k, first)
        for k in range(1, NODES):
            last = jnp.where(parent_ref[k] == m, k, last)
        return first, last

    loads[0].wait()

    @pl.when(n < 8)
    def _():
        for i in range(w):
            spread(s_r, i, t_ref[part(i), :].T)

    for i in range(w):
        spread(s_l, i, t_ref[part(i), :])
    pl.semaphore_wait(barrier, greetings)

    @pl.when(n < 8)
    def _():
        a2a_start(A2A_R, s_r, t_r)

    a2a_start(A2A_L, s_l, t_l)
    for load in loads[1:]:
        load.wait()
    left_child, right_child = family(n)
    mine = parent_ref[n]
    eldest, _ = family(mine)
    side_of = jnp.where(eldest == n, 0, 1)
    first_id = assign_ref[0, n]
    second_id = assign_ref[1, n]
    op_p = ops_ref[first_id]
    op_q = ops_ref[second_id]
    for i in range(w):
        t = t_ref[part(i), :]
        tq = exact(t, op_q)
        v = jnp.where(leaf, t + tq, tq)
        spread(s_k, i, exact(op_p, v) + jnp.where(leaf, tq, 0.0))
    a2a_start(A2A_K, s_k, k_l)

    def right_forms():
        a2a_wait(A2A_R, t_r)
        for i in range(w):
            x = t_r[i].T
            rt[i] = x
            rtc[part(i), :] = beside(x)
        for i in range(w):
            rc[part(i), :] = beside(t_r[i])

    def left_forms():
        a2a_wait(A2A_L, t_l)
        for i in range(w):
            x = t_l[i].T
            lt[i] = x
            ltc[part(i), :] = beside(x)
        for i in range(w):
            lc[part(i), :] = beside(t_l[i])

    def own_forms():
        for i in range(w):
            tc[part(i), :] = beside(t_ref[part(i), :])

    def pair_square():
        a2a_wait(A2A_K, k_l)
        total = jnp.zeros((b, b), F32)
        for i in range(w):
            total = total + exact(k_l[i], t_l[i], nt=True)
        up[...] = total

    def pick_d(count):
        arrived(NODE_D, d_cand.at[pl.ds(0, count)])
        dd_row[...] = d_cand[mine, side_of]
        slab_start(AG_D, lambda j: dd_row, dd.at[rows, :])
        dd[rows, :] = dd_row[...]

    def gather_d():
        arrived(AG_D, dd.at[other_rows, :])

    def push_d():
        slab_start(RS_D, lambda j: dp.at[:, block(j), :], rs_d.at[s])
        rs_d[s] = dp[:, rows, :]

    def square_d():
        d = dd[...]
        dp[0] = sandwich(rtc, rc, d)
        dp[1] = sandwich(ltc, lc, d)
        push_d()

    def send_d():
        arrived(RS_D, rs_d.at[others])
        total = rs_d[0]
        for k in range(1, ns):
            total = total + rs_d[k]
        d_row[...] = total
        node_start(NODE_D, d_row, d_cand.at[n], c0, c1)

    def push_u():
        slab_start(RS_U, lambda j: up.at[block(owned(n, j)), :], rs_u.at[s])
        rs_u[s] = up[block(owned(n, s)), :]

    def send_u():
        arrived(RS_U, rs_u.at[others])
        total = rs_u[0]
        for k in range(1, ns):
            total = total + rs_u[k]
        u_row[...] = total
        node_start(NODE_U, u_row, u_cand.at[n], p0, p1, owned(n, s))

    def spread_u():
        slab_start(AG_U, lambda j: xy_row, xy.at[:, rows, :])
        xy[:, rows, :] = xy_row[...]

    def pick_u(count):
        arrived(NODE_U, u_cand.at[pl.ds(0, count)])
        xy_row[0] = u_cand[left_child]
        xy_row[1] = u_cand[right_child]
        spread_u()

    def push_merged():
        slot = jnp.where(n == 3, 1, 0)

        def go(k, c):
            j = lax.rem(s + k + ns // 2, ns)
            remote(MERGE, up.at[block(j), :], m_u.at[slot, s], n // 2, j, MERGE + slot).start()
            return c

        lax.fori_loop(0, ns, go, 0)

    def pick_merged(slot):
        arrived(MERGE + slot, m_u.at[slot])
        total = m_u[slot, 0]
        for k in range(1, ns):
            total = total + m_u[slot, k]
        xy_row[slot] = total

    def gather_u():
        arrived(AG_U, xy.at[:, other_rows, :])

    def square_u():
        up[...] = up[...] + (sandwich(rc, rtc, xy[0]) + sandwich(lc, ltc, xy[1], add=k_l))

    def move_left():
        x = above(xy[0])
        for i in range(w):
            spread(s_x, i, product(x, tc[part(i), :]))
        a2a_start(A2A_X, s_x, x_l)

    def push_energy(square):
        terms = dd[...] * square
        total = terms[0:w, :]
        for k in range(1, ns):
            total = total + terms[k * w : (k + 1) * w, :]
        rs_e[s] = total
        slab_start(SLAB_E, lambda j: rs_e.at[s], rs_e.at[s])

    def own_energy():
        arrived(SLAB_E, rs_e.at[others])
        total = rs_e[0]
        for k in range(1, ns):
            total = total + rs_e[k]
        return total

    def wait_total():
        arrived(NODE_F, e_all)

    def drain_first():
        a2a_drain(A2A_L, s_l)
        a2a_drain(A2A_K, s_k)

        @pl.when(n < 8)
        def _():
            a2a_drain(A2A_R, s_r)

    factor = b**0.75

    @pl.when(leaf)
    def _():
        a2a_wait(A2A_L, t_l)
        pair_square()
        push_u()
        send_u()
        drain_first()
        pick_d(4)
        gather_d()

    @pl.when((n >= 4) & (n < 8))
    def _():
        right_forms()
        left_forms()
        pair_square()
        own_forms()
        pick_u(8)
        gather_u()
        square_u()
        push_u()
        send_u()
        move_left()
        drain_first()
        pick_d(2)
        gather_d()
        square_d()
        send_d()
        wait_total()
        node_start(NODE_F, e_all, e_all, 2 * n, 2 * n + 2)

    @pl.when((n == 2) | (n == 3))
    def _():
        right_forms()
        left_forms()
        pair_square()
        own_forms()
        drain_first()
        pick_d(1)
        gather_d()
        pick_u(4)
        square_d()
        gather_u()
        square_u()
        push_merged()
        send_d()
        push_energy(up[...])
        move_left()
        e_row[...] = own_energy()
        e_cand[n] = e_row[...]
        node_start(NODE_E, e_row, e_cand.at[n], 5 - n, 6 - n)
        arrived(NODE_E, e_cand.at[pl.ds(0, 2)])
        e_all[...] = e_cand[1] + (e_cand[2] + e_cand[3])

        @pl.when(n == 2)
        def _():
            node_start(NODE_F, e_all, e_all, 4, 8)
            node_start(NODE_F, e_all, e_all, 1, 2)

    @pl.when(n == 1)
    def _():
        right_forms()
        left_forms()
        pick_d(1)
        gather_d()
        d = dd[...]
        dp[0] = exact_sandwich(rt, d)
        dp[1] = exact_sandwich(lt, d)
        push_d()
        send_d()
        pair_square()
        push_energy(up[...])
        own_forms()
        own = own_energy()
        arrived(NODE_E, e_cand.at[0])
        e_row[...] = own + e_cand[0]
        node_start(NODE_E, e_row, e_cand.at[n], 2, 4)
        drain_first()
        pick_merged(0)
        pick_merged(1)
        spread_u()
        gather_u()
        square_u()
        push_merged()
        move_left()
        wait_total()
        node_start(NODE_F, e_all, e_all, 0, 1)

    @pl.when(n == 0)
    def _():
        chips = ns // 2
        chip, core = s // 2, lax.rem(s, 2)
        near = [chip, lax.rem(chip + 2, chips), lax.rem(chip + chips - 2, chips)]
        z_peer = s + 2 - 4 * lax.rem(chip, 2)
        holders = [s, z_peer, lax.rem(s + chips, ns), lax.rem(z_peer + chips, ns)]
        kept = len(holders)

        dd[...] = env_ref[...]
        right_forms()
        dp[0] = exact_sandwich(rt, env_ref[...])
        dp[1] = jnp.zeros((b, b), F32)
        push_d()
        send_d()
        left_forms()
        d = above(env_ref[...] * factor)
        for i in range(w):
            x_l[i] = product(d, lc[part(i), :])
        slab_start(A2A_Z, lambda j: x_l.at[:, block(j), :], z.at[0, rows])
        z[0, rows] = x_l[:, rows, :]
        pair_square()
        push_energy(up[...] + sandwich(lc, ltc, op_q))
        e_row[...] = own_energy()
        node_start(NODE_E, e_row, e_cand.at[n], 1, 2)
        arrived(A2A_Z, z.at[0, other_rows])
        for k in (3, 2, 1):
            remote(COPIES, z.at[0], z.at[k], n, holders[k]).start()
        q_side = beside(op_q)
        q_weights = jnp.concatenate([q_side, q_side], axis=0)
        same = lax.broadcasted_iota(jnp.int32, (b, b), 0) == lax.broadcasted_iota(jnp.int32, (b, b), 1)
        p_one[...] = op_p + jnp.where(same, 1.0, 0.0)

        def chip_rows(m):
            return pl.ds(pl.multiple_of(m * (2 * w), 2 * w), 2 * w)

        p_near = above(jnp.concatenate([p_one[chip_rows(m), :] for m in near], axis=0))
        drain_first()
        drained(A2A_Z, x_l.at[:, other_rows, :])
        drained(RS_D, dp.at[:, other_rows, :])
        drained(NODE_D, d_row)
        drained(SLAB_E, rs_e.at[others])
        drained(NODE_E, e_row)

        def known(q, c):
            side = beside(z.reshape(kept * b * w, b)[pl.ds((q // w) * (b * w) + lax.rem(q, w), b, stride=w), :])
            zc[q] = side
            moved = dot(side, q_weights)
            base[q] = product(p_near, beside(moved[:, :b] + moved[:, b:]))
            return c

        lax.fori_loop(0, w, known, 0)
        arrived(COPIES, z.at[pl.ds(1, kept - 1)])
        drained(COPIES, z.at[pl.ds(1, kept - 1)])
        lax.fori_loop(w, kept * w, known, 0)

        pick_merged(0)
        mine_at = pl.ds(pl.multiple_of(core * w, w), w)
        ahead_at = pl.ds(pl.multiple_of((core + 4) * w, w), w)
        behind_at = pl.ds(pl.multiple_of((core + 2) * w, w), w)
        for c in range(2):
            remote(AG_U, xy_row.at[0], x_near.at[ahead_at, :], n, 2 * near[1] + c).start()
            remote(AG_U, xy_row.at[0], x_near.at[behind_at, :], n, 2 * near[2] + c).start()
        remote(AG_U, xy_row.at[0], x_near.at[mine_at, :], n, s + 1 - 2 * core).start()
        x_near[mine_at, :] = xy_row[0]
        arrived(AG_U, x_near.at[pl.ds(0, 5 * w), :])
        x = above(x_near[...])
        x_own = above(x_near[0 : 2 * w, :])

        def span(m):
            return pl.ds(pl.multiple_of(m * w, w), w)

        for k in range(kept):
            count = 6 if k < 2 else 2
            for i in range(w):
                q = k * w + i
                g = product(x if k < 2 else x_own, zc[q]) + base[q, 0 : count * w, :]
                for t in range(count):
                    gb[t, q] = g[t * w : (t + 1) * w, :]
            for t in range(2, count):
                remote(A2A_X, gb.at[t, pl.ds(k * w, w)], out_ref.at[span(holders[k])], n, 2 * near[t // 2] + t % 2).start()
        for k in range(kept):
            remote(A2A_X, gb.at[1 - core, pl.ds(k * w, w)], out_ref.at[span(holders[k])], n, s + 1 - 2 * core).start()
            out_ref[span(holders[k])] = gb[core, pl.ds(k * w, w)]
        wait_total()
        drained(AG_U, x_near.at[pl.ds(0, 5 * w), :])
        arrived(A2A_X, out_ref.at[pl.ds(0, 12 * w)])
        drained(A2A_X, out_ref.at[pl.ds(0, 12 * w)])

    @pl.when(n >= 1)
    def _():
        @pl.when(n < 8)
        def _():
            a2a_wait(A2A_X, x_l)

        d = above(dd[...] * factor)
        for i in range(w):
            side = beside(k_l[i] + jnp.where(n < 8, x_l[i], 0.0))
            out_ref.reshape(b * w, b)[pl.ds(i, b, stride=w), :] = product(d, side)

    @pl.when(leaf)
    def _():
        wait_total()

    en_ref[...] = jnp.sum(e_all[...], axis=(0, 1), keepdims=True)

    @pl.when((n >= 1) & (n < 8))
    def _():
        a2a_drain(A2A_X, s_x)
        drained(RS_D, dp.at[:, other_rows, :])
        drained(AG_U, xy.at[:, other_rows, :])

    @pl.when(n >= 1)
    def _():
        drained(AG_D, dd.at[other_rows, :])

    @pl.when(n >= 4)
    def _():
        drained(RS_U, up.at[other_rows, :])

    @pl.when((n >= 1) & (n < 4))
    def _():
        drained(MERGE, up)
        drained(SLAB_E, rs_e.at[others])

    @pl.when(n == 1)
    def _():
        drained(NODE_D, d_cand.at[pl.ds(0, 2)])
        drained(NODE_E, e_cand.at[pl.ds(0, 2)])
        drained(NODE_F, e_all)

    @pl.when((n == 2) | (n == 3))
    def _():
        drained(NODE_D, d_cand.at[pl.ds(0, 4)])
        drained(NODE_E, e_row)

    @pl.when(n == 2)
    def _():
        drained(NODE_F, e_cand.at[pl.ds(0, 5)])

    @pl.when((n >= 4) & (n < 8))
    def _():
        drained(NODE_D, d_cand.at[pl.ds(0, 8)])
        drained(NODE_U, u_cand.at[pl.ds(0, 2)])
        drained(NODE_F, e_cand.at[pl.ds(0, 2)])

    @pl.when(leaf)
    def _():
        drained(NODE_U, u_cand.at[pl.ds(0, 4)])


def per_device(ns, tensors, ops, assign, parent, env):
    b = env.shape[0]
    w = b // ns
    stack = pltpu.VMEM((w * b, b), F32)
    full = pltpu.VMEM((b, w, b), F32)
    form = pltpu.VMEM((w, b, b), F32)
    cat = pltpu.VMEM((w * b, 2 * b), BF16)
    square = pltpu.VMEM((b, b), F32)
    slab = pltpu.VMEM((w, b), F32)
    two = pltpu.VMEM((2, w, b), F32)
    hbm = pl.BlockSpec(memory_space=pl.ANY)
    vmem = pl.BlockSpec(memory_space=pltpu.VMEM)
    grad, energy = pl.pallas_call(
        functools.partial(kernel, ns),
        out_shape=(pltpu.VMEM((b, w, b), F32), pltpu.VMEM((1, 1), F32)),
        in_specs=[hbm] * 5,
        out_specs=(vmem, vmem),
        scratch_shapes=[
            stack, pltpu.VMEM(ops.shape, F32), square,
            pltpu.SMEM((2, NODES), jnp.int32), pltpu.SMEM((NODES,), jnp.int32), pltpu.SemaphoreType.DMA((5,)),
            full, full, full, full, form, form, form, form, form, form,
            cat, cat, cat, cat, cat, pltpu.VMEM((2, ns, w, b), F32),
            square, pltpu.VMEM((ns, w, b), F32), slab, pltpu.VMEM((NODES, w, b), F32), two, pltpu.VMEM((2, b, b), F32),
            pltpu.VMEM((2, b, b), F32), pltpu.VMEM((ns, 2, w, b), F32), two,
            pltpu.VMEM((NODES, 2, w, b), F32), slab, square,
            pltpu.VMEM((ns, w, b), F32), slab, pltpu.VMEM((NODES, w, b), F32), slab,
            pltpu.VMEM((4, b, w, b), F32), pltpu.VMEM((4 * w, b, 2 * b), BF16), pltpu.VMEM((4 * w, 6 * w, b), F32),
            pltpu.VMEM((6, 4 * w, w, b), F32), pltpu.VMEM((6 * w, b), F32), square,
            pltpu.SemaphoreType.DMA((COUNT,)), pltpu.SemaphoreType.DMA((COUNT,)),
        ],
        compiler_params=pltpu.CompilerParams(collective_id=0, has_side_effects=True),
    )(tensors.reshape(w * b, b), ops, env, assign.T, parent)
    return grad[None], energy[0, 0]


def solution(mesh):
    return jax.shard_map(
        functools.partial(per_device, mesh.shape["slab"]),
        mesh=mesh,
        in_specs=(P("node", "slab", None, None), P(), P(), P(), P()),
        out_specs=(P("node", None, "slab", None), P()),
        check_vma=False,
    )
```
